256 devices in a mesh: dp: 16 (over y, z_lo, core), owner: 16 (over x, z_hi).
Axes of the slice: x: 4, y: 4, z: 8 (z_hi: 4, z_lo: 2; z = z_hi * 2 + z_lo), core: 2. Of those that a mesh axis runs over, the one named last changes fastest.
Arguments:
- tokens: bfloat16 [8192, 4096], P('dp'), may hold values from -6 to 6
- route: int32 [8192, 1], P('dp'), may hold values from 0 to 3; in each aligned block of 512 rows (0 to 511, 512 to 1023, ...) at most 384 rows name the same one
- gate_prob: float32 [8192], P('dp'), may hold values from 0.1 to 1
- w_gate: bfloat16 [4096, 6144], P('dp', 'owner'), may hold values from -0.09375 to 0.09375
- w_up: bfloat16 [4096, 6144], P('dp', 'owner'), may hold values from -0.09375 to 0.09375
- w_down: bfloat16 [6144, 4096], P('owner', 'dp'), may hold values from -0.15625 to 0.15625
- d_out: bfloat16 [8192, 4096], P('dp', 'owner'), may hold values from -1.5 to 1.5
Outputs:
- mixed: bfloat16 [8192, 4096], P('dp', 'owner')
- grad_tokens: bfloat16 [8192, 4096], P('dp', 'owner')
- grad_gate: float32 [8192], P('dp')
- grad_w_gate: float32 [4096, 6144], P('dp', 'owner')
- grad_w_up: float32 [4096, 6144], P('dp', 'owner')
- grad_w_down: float32 [6144, 4096], P('owner', 'dp')
The draws below stay inside these ranges and needn't reach their ends.
Inputs may be any that keep to these rules, and one draw needn't show every extreme that they name: `route`: in every aligned block of 512 rows no expert is named by more than 384 rows, and in some block one expert is named by exactly 384 rows.
All inputs are finite; a program needn't handle non-finite values.
Results may differ from the reference program's by a relative error of at most 0.017.
Values may be sent and summed in bfloat16 or wider, within the bound.
A program may use at most 128 MiB of HBM per device.

```python
import math
import jax
import jax.numpy as jnp
import numpy as np
from jax import lax

D = 4096
FF = 1536
EXPERTS = 4
TOK_GRP = 512
CAP = 384
TOKENS = 8192
N_DP = 16
N_OWNER = 16


def level_of(rng, shape, cuts, smallest, top_value):
    factor_of = 1.0
    for axis_at, parts in cuts:
        draws = jax.random.uniform(jax.random.fold_in(jax.random.fold_in(rng, 6), axis_at), (parts,), jnp.float32, smallest / len(cuts), top_value / len(cuts))
        factor_of = factor_of * jnp.repeat(jnp.exp(draws), shape[axis_at] // parts).reshape((-1,) + (1,) * (len(shape) - 1 - axis_at))
    return factor_of


def shared_out(own_key, own, number, rows, amount, top, bound, lean):
    order = jax.random.permutation(own_key, amount)
    packed, ordinary = load_shares(amount, rows * top, bound, lean, True), load_shares(amount, rows * top, bound, lean, False)
    places = jnp.arange(amount)

    def named(lengths, rotation):
        used = int((lengths > 0).sum())
        fixed = max(1, used // 4)
        moved = fixed + (places - fixed + rotation * (used - fixed)) % max(1, amount - fixed)
        return jnp.zeros((amount,), jnp.int32).at[order[jnp.where(places < fixed, places, moved)]].set(jnp.asarray(lengths, jnp.int32))

    lengths = jnp.where(number % 4 == 0, named(packed, number // 4), named(ordinary, number - number // 4 - 1))
    mixed = jax.random.permutation(jax.random.fold_in(own, 3), amount)
    donor, taker = mixed[0:amount // 2 * 2:2], mixed[1:amount // 2 * 2:2]
    margin = jnp.minimum(lengths[donor] - 1, bound - lengths[taker]) // 2
    margin = jnp.where((donor == order[0]) | (taker == order[0]) | (lengths[taker] == 0), 0, jnp.maximum(margin, 0))
    moved = jax.random.randint(jax.random.fold_in(own, 4), (amount // 2,), 0, 1 << 20) % (margin + 1)
    lengths = lengths.at[donor].add(-moved).at[taker].add(moved)
    labels = jnp.searchsorted(jnp.cumsum(lengths), jnp.arange(rows * top), side="right").astype(jnp.int32)
    grid = labels.reshape(top, rows).T
    grid = grid[jax.random.permutation(jax.random.fold_in(own, 1), rows)]
    rotation = jax.random.randint(jax.random.fold_in(own, 2), (rows, 1), 0, top)
    return jnp.take_along_axis(grid, (jnp.arange(top)[None, :] + rotation) % top, axis=1)


def load_shares(count, total, limit, slope, full):
    portions = [(1 << 20) // math.isqrt(grade ** slope) + 1 for grade in range(1, count + 1)]
    largest = limit if full else min(limit, max(-(-total // count), total * portions[0] // sum(portions)))
    least = 1 if total - largest >= count - 1 else 0
    counts, surplus = [largest] + [least] * (count - 1), total - largest - least * (count - 1)
    while surplus > 0:
        movable = [i for i in range(1, count) if counts[i] < largest] or [i for i in range(1, count) if counts[i] < limit]
        pool, budget = sum([portions[i] for i in movable]), surplus
        for i in movable:
            more = min(limit - counts[i], max(1, budget * portions[i] // pool), surplus)
            counts[i] = counts[i] + more
            surplus = surplus - more
    return np.array(counts)


def normal_values(stream_key, extent, deviation, bound, split=(), held_as=jnp.bfloat16):
    drawn = jax.random.normal(stream_key, extent, jnp.float32) * deviation
    if len(split) > 0:
        drawn = level_of(stream_key, extent, split, -0.22, 0.18) * drawn
    return jnp.clip(drawn, min=-bound, max=bound).astype(held_as)


def setup_inputs(seed: int = 0) -> dict:
    streams_of = jax.random.split(jax.random.key(seed), 8)
    tokens = normal_values(streams_of[0], (TOKENS, D), 1.0, 6.0, ((0, 16),))
    route_keys = jax.random.split(jax.random.fold_in(streams_of[1], 1), TOKENS // TOK_GRP)
    route_turns = jax.random.permutation(jax.random.fold_in(streams_of[1], 3), TOKENS // TOK_GRP)
    route = jax.vmap(lambda own, number: shared_out(jax.random.fold_in(streams_of[1], 2), own, number, TOK_GRP, EXPERTS, 1, CAP, 2))(route_keys, route_turns).reshape((TOKENS, 1))
    gate_prob = jnp.clip(0.1 + 0.9 * jax.random.uniform(streams_of[2], (TOKENS,), jnp.float32) ** level_of(streams_of[2], (TOKENS,), ((0, 16),), -0.2, 0.2), 0.1, 1.0)
    w_gate = normal_values(streams_of[3], (D, EXPERTS * FF), D ** -0.5, 0.09375, ((0, 16), (1, 16)))
    w_up = normal_values(streams_of[4], (D, EXPERTS * FF), D ** -0.5, 0.09375, ((0, 16), (1, 16)))
    w_down = normal_values(streams_of[5], (EXPERTS * FF, D), FF ** -0.5, 0.15625, ((0, 16), (1, 16)))
    d_out = normal_values(streams_of[6], (TOKENS, D), 0.25, 1.5, ((0, 16), (1, 16)))
    return dict(tokens=tokens, route=route, gate_prob=gate_prob, w_gate=w_gate, w_up=w_up, w_down=w_down, d_out=d_out)


def rounded(value):
    return lax.optimization_barrier(value.astype(jnp.bfloat16)).astype(jnp.float32)


def reference(tokens, route, gate_prob, w_gate, w_up, w_down, d_out):
    pieces = N_OWNER // EXPERTS
    width = FF // pieces
    chosen = route[:, 0]
    dy_full = d_out.astype(jnp.float32)
    out_sum = jnp.zeros((TOKENS, D), jnp.float32)
    input_sum = jnp.zeros((TOKENS, D), jnp.float32)
    grad_gate = jnp.zeros((TOKENS,), jnp.float32)
    gate_blocks = []
    up_blocks = []
    down_blocks = []
    for expert in range(EXPERTS):
        member = chosen == expert
        row_weights = jnp.where(member, gate_prob, jnp.float32(0.0))
        gate_block = w_gate[:, expert * FF:(expert + 1) * FF]
        up_block = w_up[:, expert * FF:(expert + 1) * FF]
        down_block = w_down[expert * FF:(expert + 1) * FF, :]
        gate_pre = jnp.dot(tokens, gate_block, preferred_element_type=jnp.float32)
        up_pre = jnp.dot(tokens, up_block, preferred_element_type=jnp.float32)
        sigma = jax.nn.sigmoid(gate_pre)
        active = gate_pre * sigma
        hidden = jnp.where(member[:, None], active * up_pre, jnp.float32(0.0)).astype(jnp.bfloat16)
        expert_out = jnp.dot(hidden, down_block, preferred_element_type=jnp.float32)
        grad_gate = grad_gate + jnp.where(member, jnp.sum(dy_full * expert_out, axis=1), jnp.float32(0.0))
        d_expert = (row_weights[:, None] * dy_full).astype(jnp.bfloat16)
        d_hidden = jnp.dot(d_expert, down_block.T, preferred_element_type=jnp.float32)
        d_gate_pre = (d_hidden * up_pre * sigma * (1.0 + gate_pre * (1.0 - sigma))).astype(jnp.bfloat16)
        d_up_pre = (d_hidden * active).astype(jnp.bfloat16)
        for portion in range(pieces):
            start_col = portion * width
            end_col = start_col + width
            piece_out = jnp.dot(hidden[:, start_col:end_col], down_block[start_col:end_col, :], preferred_element_type=jnp.float32)
            out_sum = out_sum + rounded(row_weights[:, None] * piece_out)
            piece_input = jnp.dot(d_gate_pre[:, start_col:end_col], gate_block[:, start_col:end_col].T, preferred_element_type=jnp.float32)
            piece_input = piece_input + jnp.dot(d_up_pre[:, start_col:end_col], up_block[:, start_col:end_col].T, preferred_element_type=jnp.float32)
            input_sum = input_sum + rounded(piece_input)
        gate_grad = jnp.zeros((D, FF), jnp.float32)
        up_grad = jnp.zeros((D, FF), jnp.float32)
        down_grad = jnp.zeros((FF, D), jnp.float32)
        for group in range(N_DP):
            first_row = group * TOK_GRP
            last_row = first_row + TOK_GRP
            block_tokens = tokens[first_row:last_row].T
            gate_grad = gate_grad + rounded(jnp.dot(block_tokens, d_gate_pre[first_row:last_row], preferred_element_type=jnp.float32))
            up_grad = up_grad + rounded(jnp.dot(block_tokens, d_up_pre[first_row:last_row], preferred_element_type=jnp.float32))
            down_grad = down_grad + rounded(jnp.dot(hidden[first_row:last_row].T, d_expert[first_row:last_row], preferred_element_type=jnp.float32))
        gate_blocks.append(gate_grad)
        up_blocks.append(up_grad)
        down_blocks.append(down_grad)
    mixed = out_sum.astype(jnp.bfloat16)
    grad_tokens = input_sum.astype(jnp.bfloat16)
    grad_w_gate = jnp.concatenate(gate_blocks, axis=1)
    grad_w_up = jnp.concatenate(up_blocks, axis=1)
    grad_w_down = jnp.concatenate(down_blocks, axis=0)
    return (mixed, grad_tokens, grad_gate, grad_w_gate, grad_w_up, grad_w_down)
```

```python
import functools

import jax
import jax.numpy as jnp
from jax import lax
from jax.experimental import pallas as pl
from jax.experimental.pallas import tpu as pltpu
from jax.sharding import PartitionSpec as P

EXPERTS = 4
MESH = pl.DeviceIdType.MESH
VMEM_LIMIT = 60 * 1024 * 1024


def contract_rows(left, right):
    return lax.dot_general(
        left, right, (((0,), (0,)), ((), ())), preferred_element_type=jnp.float32
    )


def contract_cols(left, right):
    return lax.dot_general(
        left, right, (((1,), (1,)), ((), ())), preferred_element_type=jnp.float32
    )


def place():
    dp = lax.axis_index("dp")
    y, zl, c = dp // 4, (dp // 2) % 2, dp % 2
    return y, zl, c


def slot_of(y, zl, c):
    return (y % 4) * 4 + zl * 2 + c


def enter(targets):
    barrier = pltpu.get_barrier_semaphore()
    for target in targets:
        pl.semaphore_signal(barrier, inc=1, device_id=target, device_id_type=MESH)
    pl.semaphore_wait(barrier, len(targets))


def dp_peers():
    y, zl, c = place()
    return {
        "z": {"dp": slot_of(y, 1 - zl, c)},
        "up": {"dp": slot_of(y + 1, zl, c)},
        "down": {"dp": slot_of(y + 3, zl, c)},
        "sib": {"dp": slot_of(y, zl, 1 - c)},
    }


def gather_kernel(own, full, send_sem, recv_sem):
    y, zl, c = place()
    peers = dp_peers()
    enter(list(peers.values()))
    kinds = own.shape[0]
    mine = slot_of(y, zl, c)

    def send(w, index, slot, peer, src=None):
        copy = pltpu.make_async_remote_copy(
            src_ref=full.at[w, slot] if src is None else src,
            dst_ref=full.at[w, slot],
            send_sem=send_sem.at[w, index],
            recv_sem=recv_sem.at[w, index],
            device_id=peers[peer],
            device_id_type=MESH,
        )
        copy.start()

    def arrived(w, index, slot):
        pltpu.make_async_remote_copy(
            src_ref=full.at[w, slot],
            dst_ref=full.at[w, slot],
            send_sem=send_sem.at[w, index],
            recv_sem=recv_sem.at[w, index],
            device_id=peers["sib"],
            device_id_type=MESH,
        ).wait_recv()

    for w in range(kinds):
        send(w, 0, mine, "z", own.at[w])
        send(w, 1, mine, "up", own.at[w])
        send(w, 2, mine, "down", own.at[w])
        send(w, 3, mine, "sib", own.at[w])
    full[:, pl.ds(mine, 1)] = own[...][:, None]
    for w in range(kinds):
        partner = slot_of(y, 1 - zl, c)
        arrived(w, 0, partner)
        send(w, 4, partner, "up")
        send(w, 5, partner, "down")
        send(w, 6, partner, "sib")
    for w in range(kinds):
        arrived(w, 1, slot_of(y + 3, zl, c))
        arrived(w, 4, slot_of(y + 3, 1 - zl, c))
        send(w, 9, slot_of(y + 3, 0, c), "up")
        arrived(w, 2, slot_of(y + 1, zl, c))
        arrived(w, 5, slot_of(y + 1, 1 - zl, c))
        send(w, 12, slot_of(y + 1, 1, c), "down")
        send(w, 7, slot_of(y + 3, zl, c), "sib")
        send(w, 8, slot_of(y + 3, 1 - zl, c), "sib")
        send(w, 10, slot_of(y + 1, zl, c), "sib")
        send(w, 11, slot_of(y + 1, 1 - zl, c), "sib")
    for w in range(kinds):
        arrived(w, 9, slot_of(y + 2, 0, c))
        send(w, 13, slot_of(y + 2, 0, c), "sib")
        arrived(w, 12, slot_of(y + 2, 1, c))
        send(w, 14, slot_of(y + 2, 1, c), "sib")
    for w in range(kinds):
        for index, slot in (
            (3, slot_of(y, zl, 1 - c)),
            (6, slot_of(y, 1 - zl, 1 - c)),
            (7, slot_of(y + 3, zl, 1 - c)),
            (8, slot_of(y + 3, 1 - zl, 1 - c)),
            (10, slot_of(y + 1, zl, 1 - c)),
            (11, slot_of(y + 1, 1 - zl, 1 - c)),
            (13, slot_of(y + 2, 0, 1 - c)),
            (14, slot_of(y + 2, 1, 1 - c)),
        ):
            arrived(w, index, slot)
    for w in range(kinds):
        for index in range(15):
            pltpu.make_async_remote_copy(
                src_ref=full.at[w, mine],
                dst_ref=full.at[w, mine],
                send_sem=send_sem.at[w, index],
                recv_sem=recv_sem.at[w, index],
                device_id=peers["sib"],
                device_id_type=MESH,
            ).wait_send()


def gather_weights(own):
    kinds, rows, cols = own.shape
    return pl.pallas_call(
        gather_kernel,
        out_shape=jax.ShapeDtypeStruct((kinds, 16, rows, cols), own.dtype),
        in_specs=[pl.BlockSpec(memory_space=pltpu.VMEM)],
        out_specs=pl.BlockSpec(memory_space=pltpu.VMEM),
        scratch_shapes=[
            pltpu.SemaphoreType.DMA((kinds, 15)),
            pltpu.SemaphoreType.DMA((kinds, 15)),
        ],
        compiler_params=pltpu.CompilerParams(
            collective_id=0, has_side_effects=True, vmem_limit_bytes=VMEM_LIMIT
        ),
    )(own)


def add_rows(out, *terms):
    rows = out.shape[0]

    @pl.loop(0, rows // 64)
    def _(step):
        at = pl.ds(pl.multiple_of(step * 64, 64), 64)
        total = terms[0][at, :].astype(jnp.float32)
        for term in terms[1:]:
            total = total + term[at, :].astype(jnp.float32)
        out[at, :] = total.astype(out.dtype)


def reduce_kernel(part, out, sib, first, second, cross, send_sem, recv_sem):
    y, zl, c = place()
    peers = dp_peers()
    enter(list(peers.values()))
    kinds = part.shape[0]

    def copy(w, index, src, dst, peer):
        return pltpu.make_async_remote_copy(
            src_ref=src,
            dst_ref=dst,
            send_sem=send_sem.at[w, index],
            recv_sem=recv_sem.at[w, index],
            device_id=peers[peer],
            device_id_type=MESH,
        )

    order = [(2, 0), (2, 1), (1, 0), (1, 1), (3, 0), (3, 1), (0, 0), (0, 1)]
    for w in range(kinds):
        for index, (dy, half) in enumerate(order):
            copy(
                w, index, part.at[w, slot_of(y + dy, half, 1 - c)], sib.at[w, index], "sib"
            ).start()

    def joined(w, index):
        dy, half = order[index]
        here = part.at[w, slot_of(y + dy, half, c)]
        copy(w, index, sib.at[w, index], sib.at[w, index], "sib").wait_recv()
        return here

    for w in range(kinds):
        for index in (0, 1):
            here = joined(w, index)
            add_rows(sib.at[w, index], sib.at[w, index], here)
            copy(w, 8 + index, sib.at[w, index], first.at[w, index], ("up", "down")[index]).start()
    for w in range(kinds):
        for index in (2, 3, 4, 5):
            here = joined(w, index)
            side, half = (index - 2) // 2, index % 2
            if side == half:
                copy(w, 8 + side, sib.at[w, side], first.at[w, side], "sib").wait_recv()
                add_rows(sib.at[w, index], sib.at[w, index], here, first.at[w, side])
            else:
                add_rows(sib.at[w, index], sib.at[w, index], here)
            copy(w, 8 + index, sib.at[w, index], second.at[w, index - 2], ("up", "down")[side]).start()
    for w in range(kinds):
        for index in (2, 3, 4, 5):
            copy(w, 8 + index, sib.at[w, index], second.at[w, index - 2], "sib").wait_recv()
        for index in (6, 7):
            joined(w, index)
        away = sib.at[w, 6 + 1 - zl]
        add_rows(
            away, away, part.at[w, slot_of(y, 1 - zl, c)], second.at[w, 1 - zl], second.at[w, 3 - zl]
        )
        copy(w, 14, away, cross.at[w], "z").start()
    for w in range(kinds):
        copy(w, 14, cross.at[w], cross.at[w], "z").wait_recv()
        add_rows(
            out.at[w],
            sib.at[w, 6 + zl],
            part.at[w, slot_of(y, zl, c)],
            second.at[w, zl],
            second.at[w, 2 + zl],
            cross.at[w],
        )
    for w in range(kinds):
        for index in range(15):
            copy(w, index, cross.at[w], cross.at[w], "sib").wait_send()


def reduce_weights(part):
    kinds, _, rows, cols = part.shape
    return pl.pallas_call(
        reduce_kernel,
        out_shape=jax.ShapeDtypeStruct((kinds, rows, cols), jnp.float32),
        in_specs=[pl.BlockSpec(memory_space=pltpu.VMEM)],
        out_specs=pl.BlockSpec(memory_space=pltpu.VMEM),
        scratch_shapes=[
            pltpu.VMEM((kinds, 8, rows, cols), part.dtype),
            pltpu.VMEM((kinds, 2, rows, cols), part.dtype),
            pltpu.VMEM((kinds, 4, rows, cols), part.dtype),
            pltpu.VMEM((kinds, rows, cols), part.dtype),
            pltpu.SemaphoreType.DMA((kinds, 15)),
            pltpu.SemaphoreType.DMA((kinds, 15)),
        ],
        compiler_params=pltpu.CompilerParams(
            collective_id=1, has_side_effects=True, vmem_limit_bytes=VMEM_LIMIT
        ),
    )(part)


def local(tokens, route, gate_prob, w_gate, w_up, w_down, d_out):
    row_count = tokens.shape[0]
    capacity = 3 * row_count // 4
    pieces = lax.axis_size("owner") // EXPERTS
    expert = lax.axis_index("owner") // pieces
    d_full = lax.all_gather(d_out, "owner", axis=1, tiled=True)
    full = gather_weights(jnp.stack([w_gate, w_up, w_down.T]))
    width = w_gate.shape[1]
    full_gate, full_up, full_down = (full[i].reshape(-1, width) for i in range(3))
    selected = route[:, 0] == expert
    slot_index = jnp.cumsum(selected.astype(jnp.int32)) - 1
    slot_ids = jnp.arange(capacity, dtype=jnp.int32)
    one_hot = jnp.logical_and(slot_index[None, :] == slot_ids[:, None], selected[None, :])
    dispatch = one_hot.astype(jnp.bfloat16)
    slot_tokens = jnp.dot(dispatch, tokens, preferred_element_type=jnp.float32).astype(jnp.bfloat16)
    slot_probs = jnp.sum(jnp.where(one_hot, gate_prob[None, :], jnp.float32(0.0)), axis=1)
    gate_pre = jnp.dot(slot_tokens, full_gate, preferred_element_type=jnp.float32)
    up_pre = jnp.dot(slot_tokens, full_up, preferred_element_type=jnp.float32)
    sigma = jax.nn.sigmoid(gate_pre)
    active = gate_pre * sigma
    hidden = (active * up_pre).astype(jnp.bfloat16)
    expert_out = contract_cols(hidden, full_down)
    slot_mixed = (expert_out * slot_probs[:, None]).astype(jnp.bfloat16)
    row_terms = contract_rows(dispatch, slot_mixed).astype(jnp.bfloat16)
    mixed = lax.psum_scatter(row_terms, "owner", scatter_dimension=1, tiled=True)
    slot_cotangent = jnp.dot(dispatch, d_full, preferred_element_type=jnp.float32)
    slot_router = jnp.sum(slot_cotangent * expert_out, axis=1)
    router_terms = jnp.sum(jnp.where(one_hot, slot_router[:, None], jnp.float32(0.0)), axis=0)
    grad_gate = lax.psum(router_terms, "owner")
    d_expert = (slot_probs[:, None] * slot_cotangent).astype(jnp.bfloat16)
    d_hidden = jnp.dot(d_expert, full_down, preferred_element_type=jnp.float32)
    d_gate_pre = (d_hidden * up_pre * sigma * (1.0 + gate_pre * (1.0 - sigma))).astype(jnp.bfloat16)
    d_up_pre = (d_hidden * active).astype(jnp.bfloat16)
    slot_input = (contract_cols(d_gate_pre, full_gate) + contract_cols(d_up_pre, full_up)).astype(jnp.bfloat16)
    input_terms = contract_rows(dispatch, slot_input).astype(jnp.bfloat16)
    grad_tokens = lax.psum_scatter(input_terms, "owner", scatter_dimension=1, tiled=True)
    terms = jnp.stack(
        [
            contract_rows(slot_tokens, d_gate_pre).astype(jnp.bfloat16),
            contract_rows(slot_tokens, d_up_pre).astype(jnp.bfloat16),
            contract_rows(d_expert, hidden).astype(jnp.bfloat16),
        ]
    ).reshape(3, 16, -1, width)
    grads = reduce_weights(terms)
    return (mixed, grad_tokens, grad_gate, grads[0], grads[1], grads[2].T)


def solution(mesh):
    in_specs = (
        P("dp", None),
        P("dp", None),
        P("dp"),
        P("dp", "owner"),
        P("dp", "owner"),
        P("owner", "dp"),
        P("dp", "owner"),
    )
    out_specs = (
        P("dp", "owner"),
        P("dp", "owner"),
        P("dp"),
        P("dp", "owner"),
        P("dp", "owner"),
        P("owner", "dp"),
    )
    return jax.shard_map(local, mesh=mesh, in_specs=in_specs, out_specs=out_specs, check_vma=False)
```

```python
import jax
import jax.numpy as jnp
from jax import lax
from jax.experimental import pallas as pl
from jax.experimental.pallas import tpu as pltpu
from jax.sharding import PartitionSpec as P

MESH = pl.DeviceIdType.MESH
VMEM_LIMIT = 63 * 1024 * 1024
BF, F32 = jnp.bfloat16, jnp.float32
CAP, ROWS, CH, PW = 384, 512, 256, 384
COPIES = 120
DOWN = 2


def nn(a, b):
    return lax.dot_general(a, b, (((1,), (0,)), ((), ())), preferred_element_type=F32)


def nt(a, b):
    return lax.dot_general(a, b, (((1,), (1,)), ((), ())), preferred_element_type=F32)


def tn(a, b):
    return lax.dot_general(a, b, (((0,), (0,)), ((), ())), preferred_element_type=F32)


def add_rows(out, *terms):
    rows = out.shape[-2]

    @pl.loop(0, rows // 64)
    def _(step):
        at = pl.ds(pl.multiple_of(step * 64, 64), 64)
        total = terms[0][at, :].astype(F32)
        for term in terms[1:]:
            total = total + term[at, :].astype(F32)
        out[at, :] = total.astype(out.dtype)


def kernel(
    tokens, route, prob, w_gate, w_up, w_down, d_out,
    mixed, grad_tokens, grad_gate, grad_g, grad_u, grad_d,
    full, slots, cot_all, cot, dexp, dhid, dh_a, dh_b, gate, up, hid, dgate, dup,
    part, gt_a, gt_b, m_out, m_in, g_out, g_in,
    grads, sib, first, second, cross, down_t, down_mine, gd_out, gd_in,
    picks, weight, router, r_z, r_x,
    send_sem, recv_sem,
):
    dp, owner = lax.axis_index("dp"), lax.axis_index("owner")
    y, zl, c = dp // 4, (dp // 2) % 2, dp % 2
    zc = dp % 4
    x, zh = owner // 4, owner % 4

    def dp_at(yy, z, cc):
        return (yy % 4) * 4 + z * 2 + cc

    peers = {
        "z": {"dp": dp_at(y, 1 - zl, c)},
        "up": {"dp": dp_at(y + 1, zl, c)},
        "down": {"dp": dp_at(y + 3, zl, c)},
        "sib": {"dp": dp_at(y, zl, 1 - c)},
        "x1": {"owner": ((x + 1) % 4) * 4 + zh},
        "x2": {"owner": ((x + 2) % 4) * 4 + zh},
        "x3": {"owner": ((x + 3) % 4) * 4 + zh},
        "zn": {"owner": x * 4 + (zh + 1) % 4},
        "zp": {"owner": x * 4 + (zh + 3) % 4},
        "z2": {"owner": x * 4 + (zh + 2) % 4},
    }
    turned = {"dp": y * 4 + zh, "owner": x * 4 + zc}
    moved = zh != zc

    barrier = pltpu.get_barrier_semaphore()
    for target in peers.values():
        pl.semaphore_signal(barrier, inc=1, device_id=target, device_id_type=MESH)

    @pl.when(moved)
    def _():
        pl.semaphore_signal(barrier, inc=1, device_id=turned, device_id_type=MESH)

    pl.semaphore_wait(barrier, len(peers) + moved.astype(jnp.int32))

    ids, sent = {}, []

    def index_of(name):
        return ids.setdefault(name, len(ids))

    def describe(name, src, dst, target):
        at = index_of(name)
        return pltpu.make_async_remote_copy(
            src_ref=src,
            dst_ref=dst,
            send_sem=send_sem.at[at],
            recv_sem=recv_sem.at[at],
            device_id=target,
            device_id_type=MESH,
        )

    def send(name, src, dst, peer):
        copy = describe(name, src, dst, peers[peer])
        copy.start()
        sent.append(copy)

    def arrived(name, dst):
        describe(name, dst, dst, peers["sib"]).wait_recv()

    def spread(w, tag, slot, peer, src=None):
        here = full.at[w, slot]
        send(("w", w, tag), here if src is None else src, here, peer)

    def landed(w, tag, slot):
        arrived(("w", w, tag), full.at[w, slot])

    mine = dp_at(y, zl, c)

    def spread0(w, own):
        for tag, peer in ((0, "up"), (1, "down"), (2, "z"), (3, "sib")):
            spread(w, tag, mine, peer, own)

    def spread1(w):
        slot = dp_at(y, 1 - zl, c)
        landed(w, 2, slot)
        for tag, peer in ((4, "up"), (5, "down"), (6, "sib")):
            spread(w, tag, slot, peer)

    def spread2(w):
        landed(w, 0, dp_at(y + 3, zl, c))
        landed(w, 4, dp_at(y + 3, 1 - zl, c))
        spread(w, 9, dp_at(y + 3, 0, c), "up")
        landed(w, 1, dp_at(y + 1, zl, c))
        landed(w, 5, dp_at(y + 1, 1 - zl, c))
        spread(w, 12, dp_at(y + 1, 1, c), "down")
        spread(w, 7, dp_at(y + 3, zl, c), "sib")
        spread(w, 8, dp_at(y + 3, 1 - zl, c), "sib")
        spread(w, 10, dp_at(y + 1, zl, c), "sib")
        spread(w, 11, dp_at(y + 1, 1 - zl, c), "sib")

    def spread3(w):
        landed(w, 9, dp_at(y + 2, 0, c))
        spread(w, 13, dp_at(y + 2, 0, c), "sib")
        landed(w, 12, dp_at(y + 2, 1, c))
        spread(w, 14, dp_at(y + 2, 1, c), "sib")

    def spread4(w):
        o = 1 - c
        for tag, slot in (
            (3, dp_at(y, zl, o)),
            (6, dp_at(y, 1 - zl, o)),
            (7, dp_at(y + 3, zl, o)),
            (8, dp_at(y + 3, 1 - zl, o)),
            (10, dp_at(y + 1, zl, o)),
            (11, dp_at(y + 1, 1 - zl, o)),
            (13, dp_at(y + 2, 0, o)),
            (14, dp_at(y + 2, 1, o)),
        ):
            landed(w, tag, slot)

    def turn(name, src, dst):
        copy = describe(name, src, dst, turned)

        @pl.when(moved)
        def _():
            copy.start()

        return copy

    def turn_wait(copy, src, dst):
        @pl.when(moved)
        def _():
            copy.wait()

        @pl.when(jnp.logical_not(moved))
        def _():
            dst[...] = src[...]

    spread0(0, w_gate)
    down_t[...] = w_down[...].astype(F32).T.astype(BF)
    turn_down = turn("turn_in", down_t, down_mine)
    for step in (1, 3, 2):
        send(("d", step), d_out, cot_all.at[x], "x%d" % step)
    cot_all[x] = d_out[...]
    full[0, mine] = w_gate[...]
    full[1, mine] = w_up[...]

    chosen = route[...]
    is_expert = lax.broadcasted_iota(jnp.int32, (8, ROWS), 0) == chosen
    upto = (
        lax.broadcasted_iota(jnp.int32, (ROWS, ROWS), 0)
        <= lax.broadcasted_iota(jnp.int32, (ROWS, ROWS), 1)
    )
    one, zero = jnp.float32(1.0), jnp.float32(0.0)
    counts = nn(jnp.where(is_expert, one, zero).astype(BF), jnp.where(upto, one, zero).astype(BF))
    place = jnp.where(is_expert, counts.astype(jnp.int32) - 1, -1)
    slot_ids = lax.broadcasted_iota(jnp.int32, (CAP, ROWS), 0)
    for e in range(4):
        picks[e] = jnp.where(slot_ids == place[e : e + 1, :], one, zero).astype(BF)
    pick = picks.at[x]
    weight[...] = jnp.broadcast_to(
        jnp.sum(pick[...].astype(F32) * prob[...], axis=1, keepdims=True), (CAP, 128)
    )

    def token_slots(lo, hi):
        @pl.loop(lo, hi)
        def _(k):
            cols = pl.ds(pl.multiple_of(k * CH, CH), CH)
            slots[k] = nn(pick[...], tokens[:, cols]).astype(BF)

    def project(w, out):
        out[...] = nn(slots[0], full[w, 0])

        @pl.loop(1, 16)
        def _(k):
            out[...] += nn(slots[k], full[w, k])

    spread1(0)
    turn_wait(turn_down, down_t, down_mine)
    spread0(DOWN, down_mine)
    full[DOWN, mine] = down_mine[...]
    token_slots(0, 8)
    spread2(0)
    spread1(DOWN)
    spread0(1, w_up)
    token_slots(8, 16)
    for step in (1, 2, 3):
        arrived(("d", step), cot_all.at[(x + 4 - step) % 4])

    @pl.loop(0, 4)
    def _(i):
        value = nn(pick[...], cot_all[i])
        cot[i] = value.astype(BF)
        dexp[i] = (weight[:, 0:1] * value).astype(BF)

    spread3(0)
    spread4(0)
    spread2(DOWN)
    spread1(1)
    project(0, gate)
    spread3(DOWN)
    spread4(DOWN)

    def hidden_term(p):
        up[...] = nn(dexp[0], full[DOWN, p])

        @pl.loop(1, 4)
        def _(i):
            up[...] += nn(dexp[i], full[DOWN, 4 * i + p])

        dhid[p] = up[...].astype(BF)

    half = CAP // 2
    nxt, prv, far = (zh + 1) % 4, (zh + 3) % 4, (zh + 2) % 4
    hidden_term(far)
    send("h1n", dhid.at[far, pl.ds(0, half)], dh_a.at[0], "zn")
    send("h1p", dhid.at[far, pl.ds(half, half)], dh_a.at[1], "zp")
    hidden_term(nxt)
    spread2(1)
    hidden_term(prv)
    arrived("h1n", dh_a.at[0])
    add_rows(dhid.at[nxt, pl.ds(0, half)], dhid.at[nxt, pl.ds(0, half)], dh_a.at[0])
    send("h2n", dhid.at[nxt], dh_b.at[0], "zn")
    arrived("h1p", dh_a.at[1])
    add_rows(dhid.at[prv, pl.ds(half, half)], dhid.at[prv, pl.ds(half, half)], dh_a.at[1])
    send("h2p", dhid.at[prv], dh_b.at[1], "zp")
    hidden_term(zh)
    spread3(1)
    spread4(1)
    project(1, up)
    arrived("h2n", dh_b.at[0])
    arrived("h2p", dh_b.at[1])

    @pl.loop(0, CAP // 32)
    def _(step):
        at = pl.ds(pl.multiple_of(step * 32, 32), 32)
        g, u = gate[at, :], up[at, :]
        d = dhid[zh, at, :].astype(F32) + dh_b[0, at, :].astype(F32) + dh_b[1, at, :].astype(F32)
        s = jax.nn.sigmoid(g)
        active = g * s
        hid[zh, at, :] = (active * u).astype(BF)
        dgate[at, :] = (d * u * s * (1.0 + g * (1.0 - s))).astype(BF)
        dup[at, :] = (d * active).astype(BF)

    send("a1n", hid.at[zh], hid.at[zh], "zn")
    send("a1p", hid.at[zh], hid.at[zh], "zp")

    def input_term(d):
        @pl.loop(0, 4)
        def _(a):
            k = 4 * a + d
            part[d, a] = (nt(dgate[...], full[0, k]) + nt(dup[...], full[1, k])).astype(BF)

    def grad_term(w, core):
        @pl.loop(0, 8)
        def _(j):
            k = 2 * j + core
            if w == DOWN:
                grads[w, k] = tn(dexp[k // 4], hid[k % 4]).astype(BF)
            else:
                grads[w, k] = tn(slots[k], (dgate if w == 0 else dup)[...]).astype(BF)

    order = [(2, 0), (2, 1), (1, 0), (1, 1), (3, 0), (3, 1), (0, 0), (0, 1)]
    sides = ("up", "down")

    def grad_part(w, index, core):
        dy, z = order[index]
        return grads.at[w, dp_at(y + dy, z, core)]

    def reduce0(w):
        for index in range(8):
            send(("s", w, index), grad_part(w, index, 1 - c), sib.at[w, index], "sib")

    def reduce1(w):
        for index in (0, 1):
            here = sib.at[w, index]
            arrived(("s", w, index), here)
            add_rows(here, here, grad_part(w, index, c))
            send(("t", w, index), here, first.at[w, index], sides[index])

    def reduce2(w):
        for index in (2, 3, 4, 5):
            here = sib.at[w, index]
            arrived(("s", w, index), here)
            side, z = (index - 2) // 2, index % 2
            if side == z:
                arrived(("t", w, side), first.at[w, side])
                add_rows(here, here, grad_part(w, index, c), first.at[w, side])
            else:
                add_rows(here, here, grad_part(w, index, c))
            send(("t", w, index), here, second.at[w, index - 2], sides[side])

    def reduce3(w):
        for index in (2, 3, 4, 5):
            arrived(("t", w, index), second.at[w, index - 2])
        for index in (6, 7):
            arrived(("s", w, index), sib.at[w, index])
        away = sib.at[w, 7 - zl]
        add_rows(
            away,
            away,
            grads.at[w, dp_at(y, 1 - zl, c)],
            second.at[w, 1 - zl],
            second.at[w, 3 - zl],
        )
        send(("c", w), away, cross.at[w], "z")

    def reduce4(w, out):
        arrived(("c", w), cross.at[w])
        add_rows(
            out,
            sib.at[w, 6 + zl],
            grads.at[w, dp_at(y, zl, c)],
            second.at[w, zl],
            second.at[w, 2 + zl],
            cross.at[w],
        )

    input_term(far)
    send("g1n", part.at[far, pl.ds(0, 2)], gt_a.at[0], "zn")
    send("g1p", part.at[far, pl.ds(2, 2)], gt_a.at[1], "zp")
    grad_term(0, 1 - c)
    reduce0(0)
    input_term(nxt)
    input_term(prv)
    arrived("a1n", hid.at[prv])
    send("a2n", hid.at[prv, pl.ds(0, half)], hid.at[prv, pl.ds(0, half)], "zn")
    arrived("a1p", hid.at[nxt])
    send("a2p", hid.at[nxt, pl.ds(half, half)], hid.at[nxt, pl.ds(half, half)], "zp")
    grad_term(0, c)
    reduce1(0)
    arrived("g1n", gt_a.at[0])
    arrived("g1p", gt_a.at[1])
    for a in (0, 1):
        add_rows(part.at[nxt, a], part.at[nxt, a], gt_a.at[0, a])
        add_rows(part.at[prv, a + 2], part.at[prv, a + 2], gt_a.at[1, a])
    send("g2n", part.at[nxt], gt_b.at[0], "zn")
    send("g2p", part.at[prv], gt_b.at[1], "zp")
    grad_term(1, 1 - c)
    reduce0(1)
    grad_term(1, c)
    reduce1(1)
    reduce2(0)
    arrived("a2n", hid.at[far, pl.ds(0, half)])
    arrived("a2p", hid.at[far, pl.ds(half, half)])

    router[...] = jnp.zeros_like(router)

    @pl.loop(0, 4)
    def _(i):
        out = nt(hid[0], full[DOWN, 4 * i])
        for p in range(1, 4):
            out = out + nt(hid[p], full[DOWN, 4 * i + p])
        router[...] += jnp.broadcast_to(
            jnp.sum(cot[i].astype(F32) * out, axis=1, keepdims=True), (CAP, 128)
        )
        m_out[i] = (weight[:, 0:1] * out).astype(BF)

    for step in (1, 3, 2):
        send(("m", step), m_out.at[(x + step) % 4], m_in.at[x], "x%d" % step)
    r_z[zh] = jnp.broadcast_to(
        jnp.sum(pick[...].astype(F32) * router[:, 0:1], axis=0, keepdims=True), (8, ROWS)
    )
    for name in ("zn", "zp", "z2"):
        send(("r", name), r_z.at[zh], r_z.at[zh], name)
    m_in[x] = m_out[x]

    grad_term(DOWN, 1 - c)
    reduce0(DOWN)
    grad_term(DOWN, c)
    reduce2(1)
    reduce1(DOWN)
    input_term(zh)
    reduce3(0)
    for name, q in (("zn", prv), ("zp", nxt), ("z2", far)):
        arrived(("r", name), r_z.at[q])
    r_x[x] = r_z[0] + r_z[1] + r_z[2] + r_z[3]
    for step in (1, 3, 2):
        send(("q", step), r_x.at[x], r_x.at[x], "x%d" % step)
    reduce2(DOWN)
    reduce4(0, grad_g)
    reduce3(1)

    def back_to_rows(source, out):
        total = tn(picks[0], source[0])
        for e in range(1, 4):
            total = total + tn(picks[e], source[e])
        out[...] = total.astype(BF)

    for step in (1, 2, 3):
        arrived(("m", step), m_in.at[(x + 4 - step) % 4])
    back_to_rows(m_in, mixed)
    reduce3(DOWN)
    reduce4(1, grad_u)
    arrived("g2n", gt_b.at[0])
    arrived("g2p", gt_b.at[1])
    for step in (1, 3, 2, 0):
        a = (x + step) % 4
        add_rows(g_out.at[a], part.at[zh, a], gt_b.at[0, a], gt_b.at[1, a])
        if step:
            send(("g", step), g_out.at[a], g_in.at[x], "x%d" % step)
    g_in[x] = g_out[x]
    reduce4(DOWN, gd_out)
    turn_grad = turn("turn_out", gd_out, gd_in)
    for step in (1, 2, 3):
        arrived(("q", step), r_x.at[(x + 4 - step) % 4])
    grad_gate[...] = (r_x[0] + r_x[1] + r_x[2] + r_x[3])[0:1, :]
    turn_wait(turn_grad, gd_out, gd_in)
    grad_d[...] = gd_in[...].astype(F32).T
    for step in (1, 2, 3):
        arrived(("g", step), g_in.at[(x + 4 - step) % 4])
    back_to_rows(g_in, grad_tokens)
    for copy in sent:
        copy.wait_send()


def local(tokens, route, gate_prob, w_gate, w_up, w_down, d_out):
    vmem = pl.BlockSpec(memory_space=pltpu.VMEM)
    weights = (CH, PW)
    square = (CAP, PW)
    block = (CAP, CH)
    mixed, grad_tokens, grad_gate, grad_g, grad_u, grad_d = pl.pallas_call(
        kernel,
        out_shape=(
            jax.ShapeDtypeStruct((ROWS, CH), BF),
            jax.ShapeDtypeStruct((ROWS, CH), BF),
            jax.ShapeDtypeStruct((1, ROWS), F32),
            jax.ShapeDtypeStruct((CH, PW), F32),
            jax.ShapeDtypeStruct((CH, PW), F32),
            jax.ShapeDtypeStruct((PW, CH), F32),
        ),
        in_specs=[vmem] * 7,
        out_specs=(vmem,) * 6,
        scratch_shapes=[
            pltpu.VMEM((3, 16, *weights), BF),
            pltpu.VMEM((16, *block), BF),
            pltpu.VMEM((4, ROWS, CH), BF),
            pltpu.VMEM((4, *block), BF),
            pltpu.VMEM((4, *block), BF),
            pltpu.VMEM((4, *square), BF),
            pltpu.VMEM((2, CAP // 2, PW), BF),
            pltpu.VMEM((2, *square), BF),
            pltpu.VMEM(square, F32),
            pltpu.VMEM(square, F32),
            pltpu.VMEM((4, *square), BF),
            pltpu.VMEM(square, BF),
            pltpu.VMEM(square, BF),
            pltpu.VMEM((4, 4, *block), BF),
            pltpu.VMEM((2, 2, *block), BF),
            pltpu.VMEM((2, 4, *block), BF),
            pltpu.VMEM((4, *block), BF),
            pltpu.VMEM((4, *block), BF),
            pltpu.VMEM((4, *block), BF),
            pltpu.VMEM((4, *block), BF),
            pltpu.VMEM((3, 16, *weights), BF),
            pltpu.VMEM((3, 8, *weights), BF),
            pltpu.VMEM((3, 2, *weights), BF),
            pltpu.VMEM((3, 4, *weights), BF),
            pltpu.VMEM((3, *weights), BF),
            pltpu.VMEM(weights, BF),
            pltpu.VMEM(weights, BF),
            pltpu.VMEM(weights, BF),
            pltpu.VMEM(weights, BF),
            pltpu.VMEM((4, CAP, ROWS), BF),
            pltpu.VMEM((CAP, 128), F32),
            pltpu.VMEM((CAP, 128), F32),
            pltpu.VMEM((4, 8, ROWS), F32),
            pltpu.VMEM((4, 8, ROWS), F32),
            pltpu.SemaphoreType.DMA((COPIES,)),
            pltpu.SemaphoreType.DMA((COPIES,)),
        ],
        compiler_params=pltpu.CompilerParams(
            collective_id=0, has_side_effects=True, vmem_limit_bytes=VMEM_LIMIT
        ),
    )(tokens, route.reshape(1, ROWS), gate_prob.reshape(1, ROWS), w_gate, w_up, w_down, d_out)
    return (mixed, grad_tokens, grad_gate.reshape(ROWS), grad_g, grad_u, grad_d)


def solution(mesh):
    in_specs = (
        P("dp", None),
        P("dp", None),
        P("dp"),
        P("dp", "owner"),
        P("dp", "owner"),
        P("owner", "dp"),
        P("dp", "owner"),
    )
    out_specs = (
        P("dp", "owner"),
        P("dp", "owner"),
        P("dp"),
        P("dp", "owner"),
        P("dp", "owner"),
        P("owner", "dp"),
    )
    return jax.shard_map(local, mesh=mesh, in_specs=in_specs, out_specs=out_specs, check_vma=False)
```

```python
import jax
import jax.numpy as jnp
from jax import lax
from jax.experimental import pallas as pl
from jax.experimental.pallas import tpu as pltpu
from jax.sharding import PartitionSpec as P

MESH = pl.DeviceIdType.MESH
VMEM_LIMIT = 63 * 1024 * 1024
BF, F32 = jnp.bfloat16, jnp.float32
CAP, ROWS, CH, PW = 384, 512, 256, 384
COPIES = 136
DOWN = 2


def nn(a, b):
    return lax.dot_general(a, b, (((1,), (0,)), ((), ())), preferred_element_type=F32)


def nt(a, b):
    return lax.dot_general(a, b, (((1,), (1,)), ((), ())), preferred_element_type=F32)


def tn(a, b):
    return lax.dot_general(a, b, (((0,), (0,)), ((), ())), preferred_element_type=F32)


def add_rows(out, *terms):
    rows = out.shape[-2]

    @pl.loop(0, rows // 64)
    def _(step):
        at = pl.ds(pl.multiple_of(step * 64, 64), 64)
        total = terms[0][at, :].astype(F32)
        for term in terms[1:]:
            total = total + term[at, :].astype(F32)
        out[at, :] = total.astype(out.dtype)


def kernel(
    tokens, route, prob, w_gate, w_up, w_down, d_out,
    mixed, grad_tokens, grad_gate, grad_g, grad_u, grad_d,
    full, slots, cot_all, cot, dexp, dhid, dh_a, dh_b, gate, up, hid, dgate, dup,
    part, g_in, in_rows, gz_a, gz_b, m_out, m_in,
    grads, sib, first, second, cross, down_t, down_mine, gd_out, gd_in,
    picks, weight, router, r_z, r_x,
    send_sem, recv_sem,
):
    dp, owner = lax.axis_index("dp"), lax.axis_index("owner")
    y, zl, c = dp // 4, (dp // 2) % 2, dp % 2
    zc = dp % 4
    x, zh = owner // 4, owner % 4

    def dp_at(yy, z, cc):
        return (yy % 4) * 4 + z * 2 + cc

    peers = {
        "z": {"dp": dp_at(y, 1 - zl, c)},
        "up": {"dp": dp_at(y + 1, zl, c)},
        "down": {"dp": dp_at(y + 3, zl, c)},
        "sib": {"dp": dp_at(y, zl, 1 - c)},
        "x1": {"owner": ((x + 1) % 4) * 4 + zh},
        "x2": {"owner": ((x + 2) % 4) * 4 + zh},
        "x3": {"owner": ((x + 3) % 4) * 4 + zh},
        "zn": {"owner": x * 4 + (zh + 1) % 4},
        "zp": {"owner": x * 4 + (zh + 3) % 4},
        "z2": {"owner": x * 4 + (zh + 2) % 4},
    }
    turned = {"dp": y * 4 + zh, "owner": x * 4 + zc}
    moved = zh != zc

    barrier = pltpu.get_barrier_semaphore()
    for target in peers.values():
        pl.semaphore_signal(barrier, inc=1, device_id=target, device_id_type=MESH)

    @pl.when(moved)
    def _():
        pl.semaphore_signal(barrier, inc=1, device_id=turned, device_id_type=MESH)

    pl.semaphore_wait(barrier, len(peers) + moved.astype(jnp.int32))

    ids, sent = {}, []

    def index_of(name):
        return ids.setdefault(name, len(ids))

    def describe(name, src, dst, target):
        at = index_of(name)
        return pltpu.make_async_remote_copy(
            src_ref=src,
            dst_ref=dst,
            send_sem=send_sem.at[at],
            recv_sem=recv_sem.at[at],
            device_id=target,
            device_id_type=MESH,
        )

    def send(name, src, dst, peer):
        copy = describe(name, src, dst, peers[peer])
        copy.start()
        sent.append(copy)

    def arrived(name, dst):
        describe(name, dst, dst, peers["sib"]).wait_recv()

    def spread(w, tag, slot, peer, src=None):
        here = full.at[w, slot]
        send(("w", w, tag), here if src is None else src, here, peer)

    def landed(w, tag, slot):
        arrived(("w", w, tag), full.at[w, slot])

    mine = dp_at(y, zl, c)

    def spread0(w, own):
        for tag, peer in ((0, "up"), (1, "down"), (2, "z"), (3, "sib")):
            spread(w, tag, mine, peer, own)

    def spread1(w):
        slot = dp_at(y, 1 - zl, c)
        landed(w, 2, slot)
        for tag, peer in ((4, "up"), (5, "down"), (6, "sib")):
            spread(w, tag, slot, peer)

    def spread2(w):
        landed(w, 0, dp_at(y + 3, zl, c))
        landed(w, 4, dp_at(y + 3, 1 - zl, c))
        spread(w, 9, dp_at(y + 3, 0, c), "up")
        landed(w, 1, dp_at(y + 1, zl, c))
        landed(w, 5, dp_at(y + 1, 1 - zl, c))
        spread(w, 12, dp_at(y + 1, 1, c), "down")
        spread(w, 7, dp_at(y + 3, zl, c), "sib")
        spread(w, 8, dp_at(y + 3, 1 - zl, c), "sib")
        spread(w, 10, dp_at(y + 1, zl, c), "sib")
        spread(w, 11, dp_at(y + 1, 1 - zl, c), "sib")

    def spread3(w):
        landed(w, 9, dp_at(y + 2, 0, c))
        spread(w, 13, dp_at(y + 2, 0, c), "sib")
        landed(w, 12, dp_at(y + 2, 1, c))
        spread(w, 14, dp_at(y + 2, 1, c), "sib")

    def from_sibling(w, dy):
        o = 1 - c
        tags = {0: (3, 6), 3: (7, 8), 1: (10, 11), 2: (13, 14)}[dy]
        halves = (0, 1) if dy == 2 else (zl, 1 - zl)
        for tag, z in zip(tags, halves):
            landed(w, tag, dp_at(y + dy, z, o))

    def turn(name, src, dst):
        copy = describe(name, src, dst, turned)

        @pl.when(moved)
        def _():
            copy.start()

        return copy

    def turn_wait(copy, src, dst):
        @pl.when(moved)
        def _():
            copy.wait()

        @pl.when(jnp.logical_not(moved))
        def _():
            dst[...] = src[...]

    spread0(0, w_gate)
    down_t[...] = w_down[...].astype(F32).T.astype(BF)
    turn_down = turn("turn_in", down_t, down_mine)
    for step in (1, 3, 2):
        send(("d", step), d_out, cot_all.at[x], "x%d" % step)
    cot_all[x] = d_out[...]
    full[0, mine] = w_gate[...]
    full[1, mine] = w_up[...]

    chosen = route[...]
    is_expert = lax.broadcasted_iota(jnp.int32, (8, ROWS), 0) == chosen
    upto = (
        lax.broadcasted_iota(jnp.int32, (ROWS, ROWS), 0)
        <= lax.broadcasted_iota(jnp.int32, (ROWS, ROWS), 1)
    )
    one, zero = jnp.float32(1.0), jnp.float32(0.0)
    counts = nn(jnp.where(is_expert, one, zero).astype(BF), jnp.where(upto, one, zero).astype(BF))
    place = jnp.where(is_expert, counts.astype(jnp.int32) - 1, -1)
    slot_ids = lax.broadcasted_iota(jnp.int32, (CAP, ROWS), 0)
    for e in range(4):
        picks[e] = jnp.where(slot_ids == place[e : e + 1, :], one, zero).astype(BF)
    pick = picks.at[x]
    weight[...] = jnp.broadcast_to(
        jnp.sum(pick[...].astype(F32) * prob[...], axis=1, keepdims=True), (CAP, 128)
    )

    def token_slots(lo, hi):
        @pl.loop(lo, hi)
        def _(k):
            cols = pl.ds(pl.multiple_of(k * CH, CH), CH)
            slots[k] = nn(pick[...], tokens[:, cols]).astype(BF)

    def project(w, out, dy):
        base = 4 * ((y + dy) % 4)
        start = nn(slots[base], full[w, base])
        out[...] = start if dy == 0 else out[...] + start

        @pl.loop(1, 4)
        def _(j):
            out[...] += nn(slots[base + j], full[w, base + j])

    turn_wait(turn_down, down_t, down_mine)
    spread0(DOWN, down_mine)
    full[DOWN, mine] = down_mine[...]
    spread1(0)
    token_slots(0, 8)
    spread1(DOWN)
    spread0(1, w_up)
    token_slots(8, 16)
    for step in (1, 2, 3):
        arrived(("d", step), cot_all.at[(x + 4 - step) % 4])

    @pl.loop(0, 4)
    def _(i):
        value = nn(pick[...], cot_all[i])
        cot[i] = value.astype(BF)
        dexp[i] = (weight[:, 0:1] * value).astype(BF)

    spread2(DOWN)
    spread2(0)
    spread1(1)
    spread3(DOWN)
    for dy in range(4):
        from_sibling(DOWN, dy)

    def hidden_term(p):
        up[...] = nn(dexp[0], full[DOWN, p])

        @pl.loop(1, 4)
        def _(i):
            up[...] += nn(dexp[i], full[DOWN, 4 * i + p])

        dhid[p] = up[...].astype(BF)

    half = CAP // 2
    nxt, prv, far = (zh + 1) % 4, (zh + 3) % 4, (zh + 2) % 4
    hidden_term(far)
    send("h1n", dhid.at[far, pl.ds(0, half)], dh_a.at[0], "zn")
    send("h1p", dhid.at[far, pl.ds(half, half)], dh_a.at[1], "zp")
    spread3(0)
    hidden_term(nxt)
    hidden_term(prv)
    arrived("h1n", dh_a.at[0])
    add_rows(dhid.at[nxt, pl.ds(0, half)], dhid.at[nxt, pl.ds(0, half)], dh_a.at[0])
    send("h2n", dhid.at[nxt], dh_b.at[0], "zn")
    arrived("h1p", dh_a.at[1])
    add_rows(dhid.at[prv, pl.ds(half, half)], dhid.at[prv, pl.ds(half, half)], dh_a.at[1])
    send("h2p", dhid.at[prv], dh_b.at[1], "zp")
    hidden_term(zh)
    for dy in (0, 3):
        from_sibling(0, dy)
        project(0, gate, dy)
    spread2(1)
    for dy in (1, 2):
        from_sibling(0, dy)
        project(0, gate, dy)
    for dy in (0, 3, 1):
        from_sibling(1, dy)
        project(1, up, dy)
    spread3(1)
    from_sibling(1, 2)
    project(1, up, 2)
    arrived("h2n", dh_b.at[0])
    arrived("h2p", dh_b.at[1])

    @pl.loop(0, CAP // 32)
    def _(step):
        at = pl.ds(pl.multiple_of(step * 32, 32), 32)
        g, u = gate[at, :], up[at, :]
        d = dhid[zh, at, :].astype(F32) + dh_b[0, at, :].astype(F32) + dh_b[1, at, :].astype(F32)
        s = jax.nn.sigmoid(g)
        active = g * s
        hid[zh, at, :] = (active * u).astype(BF)
        dgate[at, :] = (d * u * s * (1.0 + g * (1.0 - s))).astype(BF)
        dup[at, :] = (d * active).astype(BF)

    send("a1n", hid.at[zh], hid.at[zh], "zn")
    send("a1p", hid.at[zh], hid.at[zh], "zp")

    def input_term(d):
        @pl.loop(0, 4)
        def _(a):
            k = 4 * a + d
            part[d, a] = (nt(dgate[...], full[0, k]) + nt(dup[...], full[1, k])).astype(BF)

    def input_send(tag, d):
        for step in (2, 1, 3):
            send(("g", tag, step), part.at[d, (x + step) % 4], g_in.at[d, x], "x%d" % step)
        g_in[d, x] = part[d, x]

    def back_to_rows(source, out):
        total = tn(picks[0], source[0])
        for e in range(1, 4):
            total = total + tn(picks[e], source[e])
        out[...] = total.astype(BF)

    def input_rows(tag, d):
        for step in (1, 3, 2):
            arrived(("g", tag, step), g_in.at[d, (x + 4 - step) % 4])
        back_to_rows(g_in.at[d], in_rows.at[d])

    def grad_term(w, core):
        @pl.loop(0, 8)
        def _(j):
            k = 2 * j + core
            if w == DOWN:
                grads[w, k] = tn(dexp[k // 4], hid[k % 4]).astype(BF)
            else:
                grads[w, k] = tn(slots[k], (dgate if w == 0 else dup)[...]).astype(BF)

    order = [(2, 0), (2, 1), (1, 0), (1, 1), (3, 0), (3, 1), (0, 0), (0, 1)]
    sides = ("up", "down")

    def grad_part(w, index, core):
        dy, z = order[index]
        return grads.at[w, dp_at(y + dy, z, core)]

    def reduce0(w):
        for index in range(8):
            send(("s", w, index), grad_part(w, index, 1 - c), sib.at[w, index], "sib")

    def reduce1(w):
        for index in (0, 1):
            here = sib.at[w, index]
            arrived(("s", w, index), here)
            add_rows(here, here, grad_part(w, index, c))
            send(("t", w, index), here, first.at[w, index], sides[index])

    def reduce2(w):
        for index in (2, 3, 4, 5):
            here = sib.at[w, index]
            arrived(("s", w, index), here)
            side, z = (index - 2) // 2, index % 2
            if side == z:
                arrived(("t", w, side), first.at[w, side])
                add_rows(here, here, grad_part(w, index, c), first.at[w, side])
            else:
                add_rows(here, here, grad_part(w, index, c))
            send(("t", w, index), here, second.at[w, index - 2], sides[side])

    def reduce3(w):
        for index in (2, 3, 4, 5):
            arrived(("t", w, index), second.at[w, index - 2])
        for index in (6, 7):
            arrived(("s", w, index), sib.at[w, index])
        away = sib.at[w, 7 - zl]
        add_rows(
            away,
            away,
            grads.at[w, dp_at(y, 1 - zl, c)],
            second.at[w, 1 - zl],
            second.at[w, 3 - zl],
        )
        send(("c", w), away, cross.at[w], "z")

    def reduce4(w, out):
        arrived(("c", w), cross.at[w])
        add_rows(
            out,
            sib.at[w, 6 + zl],
            grads.at[w, dp_at(y, zl, c)],
            second.at[w, zl],
            second.at[w, 2 + zl],
            cross.at[w],
        )

    rh = ROWS // 2
    input_term(far)
    input_send(0, far)
    grad_term(0, 1 - c)
    reduce0(0)
    input_term(nxt)
    input_send(1, nxt)
    grad_term(0, c)
    reduce1(0)
    arrived("a1n", hid.at[prv])
    send("a2n", hid.at[prv, pl.ds(0, half)], hid.at[prv, pl.ds(0, half)], "zn")
    arrived("a1p", hid.at[nxt])
    send("a2p", hid.at[nxt, pl.ds(half, half)], hid.at[nxt, pl.ds(half, half)], "zp")
    input_term(prv)
    input_send(2, prv)
    input_rows(0, far)
    send("g1n", in_rows.at[far, pl.ds(0, rh)], gz_a.at[0], "zn")
    send("g1p", in_rows.at[far, pl.ds(rh, rh)], gz_a.at[1], "zp")
    grad_term(1, 1 - c)
    reduce0(1)
    reduce2(0)
    grad_term(1, c)
    reduce1(1)
    input_term(zh)
    input_send(3, zh)
    input_rows(1, nxt)
    arrived("g1n", gz_a.at[0])
    add_rows(in_rows.at[nxt, pl.ds(0, rh)], in_rows.at[nxt, pl.ds(0, rh)], gz_a.at[0])
    send("g2n", in_rows.at[nxt], gz_b.at[0], "zn")
    arrived("a2n", hid.at[far, pl.ds(0, half)])
    arrived("a2p", hid.at[far, pl.ds(half, half)])
    grad_term(DOWN, 1 - c)
    reduce0(DOWN)
    reduce2(1)
    grad_term(DOWN, c)
    reduce1(DOWN)
    input_rows(2, prv)
    arrived("g1p", gz_a.at[1])
    add_rows(in_rows.at[prv, pl.ds(rh, rh)], in_rows.at[prv, pl.ds(rh, rh)], gz_a.at[1])
    send("g2p", in_rows.at[prv], gz_b.at[1], "zp")

    router[...] = jnp.zeros_like(router)

    @pl.loop(0, 4)
    def _(i):
        out = nt(hid[0], full[DOWN, 4 * i])
        for p in range(1, 4):
            out = out + nt(hid[p], full[DOWN, 4 * i + p])
        router[...] += jnp.broadcast_to(
            jnp.sum(cot[i].astype(F32) * out, axis=1, keepdims=True), (CAP, 128)
        )
        m_out[i] = (weight[:, 0:1] * out).astype(BF)

    for step in (1, 3, 2):
        send(("m", step), m_out.at[(x + step) % 4], m_in.at[x], "x%d" % step)
    r_z[zh] = jnp.broadcast_to(
        jnp.sum(pick[...].astype(F32) * router[:, 0:1], axis=0, keepdims=True), (8, ROWS)
    )
    for name in ("zn", "zp", "z2"):
        send(("r", name), r_z.at[zh], r_z.at[zh], name)
    m_in[x] = m_out[x]

    reduce3(0)
    reduce2(DOWN)
    for name, q in (("zn", prv), ("zp", nxt), ("z2", far)):
        arrived(("r", name), r_z.at[q])
    r_x[x] = r_z[0] + r_z[1] + r_z[2] + r_z[3]
    for step in (1, 3, 2):
        send(("q", step), r_x.at[x], r_x.at[x], "x%d" % step)
    reduce3(1)
    reduce4(0, grad_g)
    input_rows(3, zh)
    reduce3(DOWN)
    reduce4(1, grad_u)
    for step in (1, 2, 3):
        arrived(("m", step), m_in.at[(x + 4 - step) % 4])
    back_to_rows(m_in, mixed)
    reduce4(DOWN, gd_out)
    turn_grad = turn("turn_out", gd_out, gd_in)
    for step in (1, 2, 3):
        arrived(("q", step), r_x.at[(x + 4 - step) % 4])
    grad_gate[...] = (r_x[0] + r_x[1] + r_x[2] + r_x[3])[0:1, :]
    arrived("g2n", gz_b.at[0])
    arrived("g2p", gz_b.at[1])
    add_rows(grad_tokens, in_rows.at[zh], gz_b.at[0], gz_b.at[1])
    turn_wait(turn_grad, gd_out, gd_in)
    grad_d[...] = gd_in[...].astype(F32).T
    for copy in sent:
        copy.wait_send()


def hand_over(*refs):
    n = len(refs) // 3
    ins, outs, sems = refs[:n], refs[n : 2 * n], refs[3 * n]
    held = refs[2 * n : 3 * n]
    loads = [pltpu.make_async_copy(ins[i], held[i], sems.at[0, i]) for i in range(n)]
    stores = [pltpu.make_async_copy(held[i], outs[i], sems.at[1, i]) for i in range(n)]
    for load in loads:
        load.start()
    for load, store in zip(loads, stores):
        load.wait()
        store.start()
    for store in stores:
        store.wait()


def to_outputs(arrays):
    anywhere = pl.BlockSpec(memory_space=pl.ANY)
    return pl.pallas_call(
        hand_over,
        out_shape=tuple(jax.ShapeDtypeStruct(a.shape, a.dtype) for a in arrays),
        in_specs=[anywhere] * len(arrays),
        out_specs=(anywhere,) * len(arrays),
        scratch_shapes=[pltpu.VMEM(a.shape, a.dtype) for a in arrays]
        + [pltpu.SemaphoreType.DMA((2, len(arrays)))],
        compiler_params=pltpu.CompilerParams(vmem_limit_bytes=VMEM_LIMIT),
    )(*arrays)


def local(tokens, route, gate_prob, w_gate, w_up, w_down, d_out):
    vmem = pl.BlockSpec(memory_space=pltpu.VMEM)
    weights = (CH, PW)
    square = (CAP, PW)
    block = (CAP, CH)
    results = pl.pallas_call(
        kernel,
        out_shape=(
            jax.ShapeDtypeStruct((ROWS, CH), BF),
            jax.ShapeDtypeStruct((ROWS, CH), BF),
            jax.ShapeDtypeStruct((1, ROWS), F32),
            jax.ShapeDtypeStruct((CH, PW), F32),
            jax.ShapeDtypeStruct((CH, PW), F32),
            jax.ShapeDtypeStruct((PW, CH), F32),
        ),
        in_specs=[vmem] * 7,
        out_specs=(vmem,) * 6,
        scratch_shapes=[
            pltpu.VMEM((3, 16, *weights), BF),
            pltpu.VMEM((16, *block), BF),
            pltpu.VMEM((4, ROWS, CH), BF),
            pltpu.VMEM((4, *block), BF),
            pltpu.VMEM((4, *block), BF),
            pltpu.VMEM((4, *square), BF),
            pltpu.VMEM((2, CAP // 2, PW), BF),
            pltpu.VMEM((2, *square), BF),
            pltpu.VMEM(square, F32),
            pltpu.VMEM(square, F32),
            pltpu.VMEM((4, *square), BF),
            pltpu.VMEM(square, BF),
            pltpu.VMEM(square, BF),
            pltpu.VMEM((4, 4, *block), BF),
            pltpu.VMEM((4, 4, *block), BF),
            pltpu.VMEM((4, ROWS, CH), BF),
            pltpu.VMEM((2, ROWS // 2, CH), BF),
            pltpu.VMEM((2, ROWS, CH), BF),
            pltpu.VMEM((4, *block), BF),
            pltpu.VMEM((4, *block), BF),
            pltpu.VMEM((3, 16, *weights), BF),
            pltpu.VMEM((3, 8, *weights), BF),
            pltpu.VMEM((3, 2, *weights), BF),
            pltpu.VMEM((3, 4, *weights), BF),
            pltpu.VMEM((3, *weights), BF),
            pltpu.VMEM(weights, BF),
            pltpu.VMEM(weights, BF),
            pltpu.VMEM(weights, BF),
            pltpu.VMEM(weights, BF),
            pltpu.VMEM((4, CAP, ROWS), BF),
            pltpu.VMEM((CAP, 128), F32),
            pltpu.VMEM((CAP, 128), F32),
            pltpu.VMEM((4, 8, ROWS), F32),
            pltpu.VMEM((4, 8, ROWS), F32),
            pltpu.SemaphoreType.DMA((COPIES,)),
            pltpu.SemaphoreType.DMA((COPIES,)),
        ],
        compiler_params=pltpu.CompilerParams(
            collective_id=0, has_side_effects=True, vmem_limit_bytes=VMEM_LIMIT
        ),
    )(tokens, route.reshape(1, ROWS), gate_prob.reshape(1, ROWS), w_gate, w_up, w_down, d_out)
    mixed, grad_tokens, grad_gate, grad_g, grad_u, grad_d = to_outputs(results)
    return (mixed, grad_tokens, grad_gate.reshape(ROWS), grad_g, grad_u, grad_d)


def solution(mesh):
    in_specs = (
        P("dp", None),
        P("dp", None),
        P("dp"),
        P("dp", "owner"),
        P("dp", "owner"),
        P("owner", "dp"),
        P("dp", "owner"),
    )
    out_specs = (
        P("dp", "owner"),
        P("dp", "owner"),
        P("dp"),
        P("dp", "owner"),
        P("dp", "owner"),
        P("owner", "dp"),
    )
    return jax.shard_map(local, mesh=mesh, in_specs=in_specs, out_specs=out_specs, check_vma=False)
```

```python
import jax
import jax.numpy as jnp
from jax import lax
from jax.experimental import pallas as pl
from jax.experimental.pallas import tpu as pltpu
from jax.sharding import PartitionSpec as P

MESH = pl.DeviceIdType.MESH
VMEM_LIMIT = 63 * 1024 * 1024
BF, F32 = jnp.bfloat16, jnp.float32
CAP, ROWS, CH, PW = 384, 512, 256, 384
COPIES = 236
STAGES = ((0, 256), (256, 128))
DOWN = 2


def nn(a, b):
    return lax.dot_general(a, b, (((1,), (0,)), ((), ())), preferred_element_type=F32)


def nt(a, b):
    return lax.dot_general(a, b, (((1,), (1,)), ((), ())), preferred_element_type=F32)


def add_rows(out, *terms):
    rows = out.shape[-2]

    @pl.loop(0, rows // 64)
    def _(step):
        at = pl.ds(pl.multiple_of(step * 64, 64), 64)
        total = terms[0][at, :].astype(F32)
        for term in terms[1:]:
            total = total + term[at, :].astype(F32)
        out[at, :] = total.astype(out.dtype)


def kernel(
    tokens, route, prob, w_gate, w_up, w_down, d_out,
    mixed, grad_tokens, grad_gate, grad_g, grad_u, grad_d,
    full_a, full_b, slots, cot_all, cot, dexp,
    dhid_a, dhid_b, dh_aa, dh_ab, dh_ba, dh_bb,
    gate_a, gate_b, up_a, up_b, hid_a, hid_b, dgate_a, dgate_b, dup_a, dup_b, acc_a, acc_b,
    part, g_in, in_rows, gz_a, gz_b, m_out, m_in,
    grads_a, grads_b, sib_a, sib_b, first_a, first_b, second_a, second_b, cross_a, cross_b,
    down_t, down_mine, gd_out_a, gd_out_b, gd_in_a, gd_in_b,
    picks, picks_t, slots_t, dexp_t, weight, router, r_z, r_x,
    send_sem, recv_sem,
):
    full, dhid = (full_a, full_b), (dhid_a, dhid_b)
    dh_first, dh_second = (dh_aa, dh_ab), (dh_ba, dh_bb)
    gate, up, hid = (gate_a, gate_b), (up_a, up_b), (hid_a, hid_b)
    dgate, dup, acc = (dgate_a, dgate_b), (dup_a, dup_b), (acc_a, acc_b)
    grads, sib = (grads_a, grads_b), (sib_a, sib_b)
    first, second, cross = (first_a, first_b), (second_a, second_b), (cross_a, cross_b)
    gd_out, gd_in = (gd_out_a, gd_out_b), (gd_in_a, gd_in_b)

    def columns(ref, s):
        return ref.at[:, pl.ds(*STAGES[s])]

    dp, owner = lax.axis_index("dp"), lax.axis_index("owner")
    y, zl, c = dp // 4, (dp // 2) % 2, dp % 2
    zc = dp % 4
    x, zh = owner // 4, owner % 4

    def dp_at(yy, z, cc):
        return (yy % 4) * 4 + z * 2 + cc

    peers = {
        "z": {"dp": dp_at(y, 1 - zl, c)},
        "up": {"dp": dp_at(y + 1, zl, c)},
        "down": {"dp": dp_at(y + 3, zl, c)},
        "sib": {"dp": dp_at(y, zl, 1 - c)},
        "x1": {"owner": ((x + 1) % 4) * 4 + zh},
        "x2": {"owner": ((x + 2) % 4) * 4 + zh},
        "x3": {"owner": ((x + 3) % 4) * 4 + zh},
        "zn": {"owner": x * 4 + (zh + 1) % 4},
        "zp": {"owner": x * 4 + (zh + 3) % 4},
        "z2": {"owner": x * 4 + (zh + 2) % 4},
    }
    turned = {"dp": y * 4 + zh, "owner": x * 4 + zc}
    moved = zh != zc

    barrier = pltpu.get_barrier_semaphore()
    for target in peers.values():
        pl.semaphore_signal(barrier, inc=1, device_id=target, device_id_type=MESH)

    @pl.when(moved)
    def _():
        pl.semaphore_signal(barrier, inc=1, device_id=turned, device_id_type=MESH)

    pl.semaphore_wait(barrier, len(peers) + moved.astype(jnp.int32))

    ids, sent = {}, []

    def index_of(name):
        return ids.setdefault(name, len(ids))

    def describe(name, src, dst, target):
        at = index_of(name)
        return pltpu.make_async_remote_copy(
            src_ref=src,
            dst_ref=dst,
            send_sem=send_sem.at[at],
            recv_sem=recv_sem.at[at],
            device_id=target,
            device_id_type=MESH,
        )

    def send(name, src, dst, peer):
        copy = describe(name, src, dst, peers[peer])
        copy.start()
        sent.append(copy)

    def arrived(name, dst):
        describe(name, dst, dst, peers["sib"]).wait_recv()

    def spread(w, tag, slot, peer, src=None):
        here = full[w[0]].at[w[1], slot]
        send(("w", w, tag), here if src is None else src, here, peer)

    def landed(w, tag, slot):
        arrived(("w", w, tag), full[w[0]].at[w[1], slot])

    mine = dp_at(y, zl, c)

    def spread0(w, own):
        for tag, peer in ((0, "up"), (1, "down"), (2, "z"), (3, "sib")):
            spread(w, tag, mine, peer, columns(own, w[0]))

    def spread1(w):
        slot = dp_at(y, 1 - zl, c)
        landed(w, 2, slot)
        for tag, peer in ((4, "up"), (5, "down"), (6, "sib")):
            spread(w, tag, slot, peer)

    def spread2(w):
        landed(w, 0, dp_at(y + 3, zl, c))
        landed(w, 4, dp_at(y + 3, 1 - zl, c))
        spread(w, 9, dp_at(y + 3, 0, c), "up")
        landed(w, 1, dp_at(y + 1, zl, c))
        landed(w, 5, dp_at(y + 1, 1 - zl, c))
        spread(w, 12, dp_at(y + 1, 1, c), "down")
        spread(w, 7, dp_at(y + 3, zl, c), "sib")
        spread(w, 8, dp_at(y + 3, 1 - zl, c), "sib")
        spread(w, 10, dp_at(y + 1, zl, c), "sib")
        spread(w, 11, dp_at(y + 1, 1 - zl, c), "sib")

    def spread3(w):
        landed(w, 9, dp_at(y + 2, 0, c))
        spread(w, 13, dp_at(y + 2, 0, c), "sib")
        landed(w, 12, dp_at(y + 2, 1, c))
        spread(w, 14, dp_at(y + 2, 1, c), "sib")

    def from_sibling(w, dy):
        o = 1 - c
        tags = {0: (3, 6), 3: (7, 8), 1: (10, 11), 2: (13, 14)}[dy]
        halves = (0, 1) if dy == 2 else (zl, 1 - zl)
        for tag, z in zip(tags, halves):
            landed(w, tag, dp_at(y + dy, z, o))

    def turn(name, src, dst):
        copy = describe(name, src, dst, turned)

        @pl.when(moved)
        def _():
            copy.start()

        return copy

    def turn_wait(copy, src, dst):
        @pl.when(moved)
        def _():
            copy.wait()

        @pl.when(jnp.logical_not(moved))
        def _():
            dst[...] = src[...]

    G1, U1, D1, G2, U2, D2 = [(stage, kind) for stage in (0, 1) for kind in (0, 1, DOWN)]
    spread0(G1, w_gate)
    down_t[...] = w_down[...].astype(F32).T.astype(BF)
    turn_down = turn("turn_in", down_t, down_mine)
    for step in (1, 3, 2):
        send(("d", step), d_out, cot_all.at[x], "x%d" % step)
    cot_all[x] = d_out[...]
    for stage in (0, 1):
        full[stage][0, mine] = columns(w_gate, stage)[...]
        full[stage][1, mine] = columns(w_up, stage)[...]

    chosen = route[...]
    is_expert = lax.broadcasted_iota(jnp.int32, (8, ROWS), 0) == chosen
    upto = (
        lax.broadcasted_iota(jnp.int32, (ROWS, ROWS), 0)
        <= lax.broadcasted_iota(jnp.int32, (ROWS, ROWS), 1)
    )
    one, zero = jnp.float32(1.0), jnp.float32(0.0)
    counts = nn(jnp.where(is_expert, one, zero).astype(BF), jnp.where(upto, one, zero).astype(BF))
    place = jnp.where(is_expert, counts.astype(jnp.int32) - 1, -1)
    slot_ids = lax.broadcasted_iota(jnp.int32, (CAP, ROWS), 0)
    for e in range(4):
        chosen_slots = jnp.where(slot_ids == place[e : e + 1, :], one, zero).astype(BF)
        picks[e] = chosen_slots
        picks_t[e] = chosen_slots.T
    pick = picks.at[x]
    weight[...] = jnp.broadcast_to(
        jnp.sum(pick[...].astype(F32) * prob[...], axis=1, keepdims=True), (CAP, 128)
    )

    def token_slots(lo, hi):
        @pl.loop(lo, hi)
        def _(k):
            cols = pl.ds(pl.multiple_of(k * CH, CH), CH)
            value = nn(pick[...], tokens[:, cols]).astype(BF)
            slots[k] = value
            slots_t[k] = value.T

    def project(w, dy):
        out = (gate, up)[w[1]][w[0]]
        source = full[w[0]]
        base = 4 * ((y + dy) % 4)
        start = nn(slots[base], source[w[1], base])
        out[...] = start if dy == 0 else out[...] + start

        @pl.loop(1, 4)
        def _(j):
            out[...] += nn(slots[base + j], source[w[1], base + j])

    def project_all(w):
        for dy in (0, 3, 1, 2):
            from_sibling(w, dy)
            project(w, dy)

    half = CAP // 2
    nxt, prv, far = (zh + 1) % 4, (zh + 3) % 4, (zh + 2) % 4

    def hidden_term(s, p):
        total = acc[s]
        total[...] = nn(dexp[0], full[s][DOWN, p])

        @pl.loop(1, 4)
        def _(i):
            total[...] += nn(dexp[i], full[s][DOWN, 4 * i + p])

        dhid[s][p] = total[...].astype(BF)

    def hidden0(s):
        hidden_term(s, far)
        send(("h1n", s), dhid[s].at[far, pl.ds(0, half)], dh_first[s].at[0], "zn")
        send(("h1p", s), dhid[s].at[far, pl.ds(half, half)], dh_first[s].at[1], "zp")

    def hidden1(s):
        arrived(("h1n", s), dh_first[s].at[0])
        here = dhid[s].at[nxt, pl.ds(0, half)]
        add_rows(here, here, dh_first[s].at[0])
        send(("h2n", s), dhid[s].at[nxt], dh_second[s].at[0], "zn")
        arrived(("h1p", s), dh_first[s].at[1])
        here = dhid[s].at[prv, pl.ds(half, half)]
        add_rows(here, here, dh_first[s].at[1])
        send(("h2p", s), dhid[s].at[prv], dh_second[s].at[1], "zp")

    def activate(s):
        arrived(("h2n", s), dh_second[s].at[0])
        arrived(("h2p", s), dh_second[s].at[1])

        @pl.loop(0, CAP // 32)
        def _(step):
            at = pl.ds(pl.multiple_of(step * 32, 32), 32)
            g, u = gate[s][at, :], up[s][at, :]
            d = dhid[s][zh, at, :].astype(F32)
            d = d + dh_second[s][0, at, :].astype(F32) + dh_second[s][1, at, :].astype(F32)
            sig = jax.nn.sigmoid(g)
            active = g * sig
            hid[s][zh, at, :] = (active * u).astype(BF)
            dgate[s][at, :] = (d * u * sig * (1.0 + g * (1.0 - sig))).astype(BF)
            dup[s][at, :] = (d * active).astype(BF)

        send(("a1n", s), hid[s].at[zh], hid[s].at[zh], "zn")
        send(("a1p", s), hid[s].at[zh], hid[s].at[zh], "zp")

    def pass_hidden(s):
        arrived(("a1n", s), hid[s].at[prv])
        here = hid[s].at[prv, pl.ds(0, half)]
        send(("a2n", s), here, here, "zn")
        arrived(("a1p", s), hid[s].at[nxt])
        here = hid[s].at[nxt, pl.ds(half, half)]
        send(("a2p", s), here, here, "zp")

    def all_hidden(s):
        arrived(("a2n", s), hid[s].at[far, pl.ds(0, half)])
        arrived(("a2p", s), hid[s].at[far, pl.ds(half, half)])

    def input_term(d):
        @pl.loop(0, 4)
        def _(a):
            k = 4 * a + d
            total = nt(dgate_a[...], full_a[0, k]) + nt(dup_a[...], full_a[1, k])
            total = total + nt(dgate_b[...], full_b[0, k]) + nt(dup_b[...], full_b[1, k])
            part[d, a] = total.astype(BF)

    def input_send(tag, d):
        for step in (2, 1, 3):
            send(("g", tag, step), part.at[d, (x + step) % 4], g_in.at[d, x], "x%d" % step)
        g_in[d, x] = part[d, x]

    def back_to_rows(source, out):
        total = nn(picks_t[0], source[0])
        for e in range(1, 4):
            total = total + nn(picks_t[e], source[e])
        out[...] = total.astype(BF)

    def input_rows(tag, d):
        for step in (1, 3, 2):
            arrived(("g", tag, step), g_in.at[d, (x + 4 - step) % 4])
        back_to_rows(g_in.at[d], in_rows.at[d])

    def grad_term(w, core):
        s, kind = w

        @pl.loop(0, 8)
        def _(j):
            k = 2 * j + core
            if kind == DOWN:
                grads[s][kind, k] = nn(dexp_t[k // 4], hid[s][k % 4]).astype(BF)
            else:
                grads[s][kind, k] = nn(slots_t[k], (dgate, dup)[kind][s][...]).astype(BF)

    order = [(2, 0), (2, 1), (1, 0), (1, 1), (3, 0), (3, 1), (0, 0), (0, 1)]
    sides = ("up", "down")

    def grad_part(w, index, core):
        dy, z = order[index]
        return grads[w[0]].at[w[1], dp_at(y + dy, z, core)]

    def reduce0(w):
        grad_term(w, 1 - c)
        for index in range(8):
            here = sib[w[0]].at[w[1], index]
            send(("s", w, index), grad_part(w, index, 1 - c), here, "sib")

    def reduce1(w):
        grad_term(w, c)
        for index in (0, 1):
            here = sib[w[0]].at[w[1], index]
            arrived(("s", w, index), here)
            add_rows(here, here, grad_part(w, index, c))
            send(("t", w, index), here, first[w[0]].at[w[1], index], sides[index])

    def reduce2(w):
        for index in (2, 3, 4, 5):
            here = sib[w[0]].at[w[1], index]
            arrived(("s", w, index), here)
            side, z = (index - 2) // 2, index % 2
            if side == z:
                came = first[w[0]].at[w[1], side]
                arrived(("t", w, side), came)
                add_rows(here, here, grad_part(w, index, c), came)
            else:
                add_rows(here, here, grad_part(w, index, c))
            send(("t", w, index), here, second[w[0]].at[w[1], index - 2], sides[side])

    def reduce3(w):
        s, kind = w
        for index in (2, 3, 4, 5):
            arrived(("t", w, index), second[s].at[kind, index - 2])
        for index in (6, 7):
            arrived(("s", w, index), sib[s].at[kind, index])
        away = sib[s].at[kind, 7 - zl]
        add_rows(
            away,
            away,
            grads[s].at[kind, dp_at(y, 1 - zl, c)],
            second[s].at[kind, 1 - zl],
            second[s].at[kind, 3 - zl],
        )
        send(("c", w), away, cross[s].at[kind], "z")

    def reduce4(w):
        s, kind = w
        arrived(("c", w), cross[s].at[kind])
        add_rows(
            gd_out[s] if kind == DOWN else columns((grad_g, grad_u)[kind], s),
            sib[s].at[kind, 6 + zl],
            grads[s].at[kind, dp_at(y, zl, c)],
            second[s].at[kind, zl],
            second[s].at[kind, 2 + zl],
            cross[s].at[kind],
        )
        if kind == DOWN:
            return turn(("turn_out", s), gd_out[s], gd_in[s])

    def finish_down(s, copy):
        lo, width = STAGES[s]
        turn_wait(copy, gd_out[s], gd_in[s])
        grad_d[pl.ds(lo, width), :] = gd_in[s][...].astype(F32).T

    def layer_output():
        router[...] = jnp.zeros_like(router)

        @pl.loop(0, 4)
        def _(i):
            out = nt(hid_a[0], full_a[DOWN, 4 * i]) + nt(hid_b[0], full_b[DOWN, 4 * i])
            for p in range(1, 4):
                out = out + nt(hid_a[p], full_a[DOWN, 4 * i + p])
                out = out + nt(hid_b[p], full_b[DOWN, 4 * i + p])
            router[...] += jnp.broadcast_to(
                jnp.sum(cot[i].astype(F32) * out, axis=1, keepdims=True), (CAP, 128)
            )
            m_out[i] = (weight[:, 0:1] * out).astype(BF)

        for step in (1, 3, 2):
            send(("m", step), m_out.at[(x + step) % 4], m_in.at[x], "x%d" % step)
        r_z[zh] = jnp.broadcast_to(
            jnp.sum(pick[...].astype(F32) * router[:, 0:1], axis=0, keepdims=True), (8, ROWS)
        )
        for name in ("zn", "zp", "z2"):
            send(("r", name), r_z.at[zh], r_z.at[zh], name)
        m_in[x] = m_out[x]

    turn_wait(turn_down, down_t, down_mine)
    spread0(D1, down_mine)
    for stage in (0, 1):
        full[stage][DOWN, mine] = columns(down_mine, stage)[...]
    spread1(G1)
    spread0(U1, w_up)
    token_slots(0, 8)
    spread1(D1)
    spread1(U1)
    token_slots(8, 16)
    spread2(D1)
    spread0(D2, down_mine)
    spread2(G1)
    for step in (1, 2, 3):
        arrived(("d", step), cot_all.at[(x + 4 - step) % 4])

    @pl.loop(0, 4)
    def _(i):
        value = nn(pick[...], cot_all[i])
        cot[i] = value.astype(BF)
        scaled = (weight[:, 0:1] * value).astype(BF)
        dexp[i] = scaled
        dexp_t[i] = scaled.T

    spread1(D2)
    spread0(G2, w_gate)
    spread3(D1)
    spread2(U1)
    for dy in range(4):
        from_sibling(D1, dy)
    hidden0(0)
    spread3(G1)
    hidden_term(0, nxt)
    hidden_term(0, prv)
    spread1(G2)
    spread0(U2, w_up)
    spread2(D2)
    spread3(U1)
    hidden1(0)
    project_all(G1)
    hidden_term(0, zh)
    spread1(U2)
    spread2(G2)
    project_all(U1)
    spread3(D2)
    for dy in range(4):
        from_sibling(D2, dy)
    hidden0(1)
    spread2(U2)
    hidden_term(1, nxt)
    hidden_term(1, prv)
    spread3(G2)
    activate(0)
    reduce0(G1)
    spread3(U2)
    reduce1(G1)
    hidden1(1)
    hidden_term(1, zh)
    project_all(G2)
    project_all(U2)
    activate(1)

    rh = ROWS // 2
    input_term(far)
    input_send(0, far)
    pass_hidden(0)
    reduce0(U1)
    input_term(nxt)
    input_send(1, nxt)
    reduce1(U1)
    reduce2(G1)
    pass_hidden(1)
    input_term(prv)
    input_send(2, prv)
    all_hidden(0)
    reduce0(D1)
    input_rows(0, far)
    send("g1n", in_rows.at[far, pl.ds(0, rh)], gz_a.at[0], "zn")
    send("g1p", in_rows.at[far, pl.ds(rh, rh)], gz_a.at[1], "zp")
    reduce1(D1)
    reduce2(U1)
    input_term(zh)
    input_send(3, zh)
    reduce0(G2)
    reduce1(G2)
    reduce0(U2)
    reduce1(U2)
    input_rows(1, nxt)
    arrived("g1n", gz_a.at[0])
    add_rows(in_rows.at[nxt, pl.ds(0, rh)], in_rows.at[nxt, pl.ds(0, rh)], gz_a.at[0])
    send("g2n", in_rows.at[nxt], gz_b.at[0], "zn")
    reduce3(G1)
    reduce2(D1)
    all_hidden(1)
    reduce0(D2)
    reduce1(D2)
    reduce2(G2)
    input_rows(2, prv)
    arrived("g1p", gz_a.at[1])
    add_rows(in_rows.at[prv, pl.ds(rh, rh)], in_rows.at[prv, pl.ds(rh, rh)], gz_a.at[1])
    send("g2p", in_rows.at[prv], gz_b.at[1], "zp")
    reduce3(U1)
    reduce2(U2)
    layer_output()
    reduce4(G1)
    reduce2(D2)
    reduce3(D1)
    reduce4(U1)
    for name, q in (("zn", prv), ("zp", nxt), ("z2", far)):
        arrived(("r", name), r_z.at[q])
    r_x[x] = r_z[0] + r_z[1] + r_z[2] + r_z[3]
    for step in (1, 3, 2):
        send(("q", step), r_x.at[x], r_x.at[x], "x%d" % step)
    reduce3(G2)
    turn_one = reduce4(D1)
    input_rows(3, zh)
    reduce3(U2)
    reduce4(G2)
    reduce3(D2)
    for step in (1, 2, 3):
        arrived(("m", step), m_in.at[(x + 4 - step) % 4])
    back_to_rows(m_in, mixed)
    reduce4(U2)
    turn_two = reduce4(D2)
    finish_down(0, turn_one)
    for step in (1, 2, 3):
        arrived(("q", step), r_x.at[(x + 4 - step) % 4])
    grad_gate[...] = (r_x[0] + r_x[1] + r_x[2] + r_x[3])[0:1, :]
    arrived("g2n", gz_b.at[0])
    arrived("g2p", gz_b.at[1])
    add_rows(grad_tokens, in_rows.at[zh], gz_b.at[0], gz_b.at[1])
    finish_down(1, turn_two)
    for copy in sent:
        copy.wait_send()


def hand_over(*refs):
    n = len(refs) // 3
    ins, outs, sems = refs[:n], refs[n : 2 * n], refs[3 * n]
    held = refs[2 * n : 3 * n]
    loads = [pltpu.make_async_copy(ins[i], held[i], sems.at[0, i]) for i in range(n)]
    stores = [pltpu.make_async_copy(held[i], outs[i], sems.at[1, i]) for i in range(n)]
    for load in loads:
        load.start()
    for load, store in zip(loads, stores):
        load.wait()
        store.start()
    for store in stores:
        store.wait()


def to_outputs(arrays):
    anywhere = pl.BlockSpec(memory_space=pl.ANY)
    return pl.pallas_call(
        hand_over,
        out_shape=tuple(jax.ShapeDtypeStruct(a.shape, a.dtype) for a in arrays),
        in_specs=[anywhere] * len(arrays),
        out_specs=(anywhere,) * len(arrays),
        scratch_shapes=[pltpu.VMEM(a.shape, a.dtype) for a in arrays]
        + [pltpu.SemaphoreType.DMA((2, len(arrays)))],
        compiler_params=pltpu.CompilerParams(vmem_limit_bytes=VMEM_LIMIT),
    )(*arrays)


def local(tokens, route, gate_prob, w_gate, w_up, w_down, d_out):
    vmem = pl.BlockSpec(memory_space=pltpu.VMEM)
    block = (CAP, CH)

    def staged(*shape, dtype=BF):
        return [pltpu.VMEM((*shape, width), dtype) for _, width in STAGES]

    results = pl.pallas_call(
        kernel,
        out_shape=(
            jax.ShapeDtypeStruct((ROWS, CH), BF),
            jax.ShapeDtypeStruct((ROWS, CH), BF),
            jax.ShapeDtypeStruct((1, ROWS), F32),
            jax.ShapeDtypeStruct((CH, PW), F32),
            jax.ShapeDtypeStruct((CH, PW), F32),
            jax.ShapeDtypeStruct((PW, CH), F32),
        ),
        in_specs=[vmem] * 7,
        out_specs=(vmem,) * 6,
        scratch_shapes=[
            *staged(3, 16, CH),
            pltpu.VMEM((16, *block), BF),
            pltpu.VMEM((4, ROWS, CH), BF),
            pltpu.VMEM((4, *block), BF),
            pltpu.VMEM((4, *block), BF),
            *staged(4, CAP),
            *staged(2, CAP // 2),
            *staged(2, CAP),
            *staged(CAP, dtype=F32),
            *staged(CAP, dtype=F32),
            *staged(4, CAP),
            *staged(CAP),
            *staged(CAP),
            *staged(CAP, dtype=F32),
            pltpu.VMEM((4, 4, *block), BF),
            pltpu.VMEM((4, 4, *block), BF),
            pltpu.VMEM((4, ROWS, CH), BF),
            pltpu.VMEM((2, ROWS // 2, CH), BF),
            pltpu.VMEM((2, ROWS, CH), BF),
            pltpu.VMEM((4, *block), BF),
            pltpu.VMEM((4, *block), BF),
            *staged(3, 16, CH),
            *staged(3, 8, CH),
            *staged(3, 2, CH),
            *staged(3, 4, CH),
            *staged(3, CH),
            pltpu.VMEM((CH, PW), BF),
            pltpu.VMEM((CH, PW), BF),
            *staged(CH),
            *staged(CH),
            pltpu.VMEM((4, CAP, ROWS), BF),
            pltpu.VMEM((4, ROWS, CAP), BF),
            pltpu.VMEM((16, CH, CAP), BF),
            pltpu.VMEM((4, CH, CAP), BF),
            pltpu.VMEM((CAP, 128), F32),
            pltpu.VMEM((CAP, 128), F32),
            pltpu.VMEM((4, 8, ROWS), F32),
            pltpu.VMEM((4, 8, ROWS), F32),
            pltpu.SemaphoreType.DMA((COPIES,)),
            pltpu.SemaphoreType.DMA((COPIES,)),
        ],
        compiler_params=pltpu.CompilerParams(
            collective_id=0, has_side_effects=True, vmem_limit_bytes=VMEM_LIMIT
        ),
    )(tokens, route.reshape(1, ROWS), gate_prob.reshape(1, ROWS), w_gate, w_up, w_down, d_out)
    mixed, grad_tokens, grad_gate, grad_g, grad_u, grad_d = to_outputs(results)
    return (mixed, grad_tokens, grad_gate.reshape(ROWS), grad_g, grad_u, grad_d)


def solution(mesh):
    in_specs = (
        P("dp", None),
        P("dp", None),
        P("dp"),
        P("dp", "owner"),
        P("dp", "owner"),
        P("owner", "dp"),
        P("dp", "owner"),
    )
    out_specs = (
        P("dp", "owner"),
        P("dp", "owner"),
        P("dp"),
        P("dp", "owner"),
        P("dp", "owner"),
        P("owner", "dp"),
    )
    return jax.shard_map(local, mesh=mesh, in_specs=in_specs, out_specs=out_specs, check_vma=False)
```

```python
import jax
import jax.numpy as jnp
from jax import lax
from jax.experimental import pallas as pl
from jax.experimental.pallas import tpu as pltpu
from jax.sharding import PartitionSpec as P

MESH = pl.DeviceIdType.MESH
VMEM_LIMIT = 63 * 1024 * 1024
BF, F32 = jnp.bfloat16, jnp.float32
CAP, ROWS, CH, PW = 384, 512, 256, 384
COPIES = 236
STAGES = ((0, 256), (256, 128))
DOWN = 2


def nn(a, b):
    return lax.dot_general(a, b, (((1,), (0,)), ((), ())), preferred_element_type=F32)


def nt(a, b):
    return lax.dot_general(a, b, (((1,), (1,)), ((), ())), preferred_element_type=F32)


def add_rows(out, *terms):
    rows = out.shape[-2]

    @pl.loop(0, rows // 64)
    def _(step):
        at = pl.ds(pl.multiple_of(step * 64, 64), 64)
        total = terms[0][at, :].astype(F32)
        for term in terms[1:]:
            total = total + term[at, :].astype(F32)
        out[at, :] = total.astype(out.dtype)


def kernel(
    tokens_hbm, route, prob, w_gate, w_up, w_down, d_out,
    mixed, grad_tokens, grad_gate, grad_g, grad_u, grad_d,
    full_a, full_b, slots, cot_all, cot, dexp,
    dhid_a, dhid_b, dh_aa, dh_ab, dh_ba, dh_bb,
    gate_a, gate_b, up_a, up_b, hid_a, hid_b, dgate_a, dgate_b, dup_a, dup_b, acc_a, acc_b,
    part, g_in, in_rows, gz_a, gz_b, m_out, m_in,
    grads_a, grads_b, sib_a, sib_b, first_a, first_b, second_a, second_b, cross_a, cross_b,
    down_t, down_mine, gd_out_a, gd_out_b, gd_in_a, gd_in_b,
    picks, picks_t, slots_t, dexp_t, weight, router, r_z, r_x,
    tokens, tokens_sem, send_sem, recv_sem,
):
    full, dhid = (full_a, full_b), (dhid_a, dhid_b)
    dh_first, dh_second = (dh_aa, dh_ab), (dh_ba, dh_bb)
    gate, up, hid = (gate_a, gate_b), (up_a, up_b), (hid_a, hid_b)
    dgate, dup, acc = (dgate_a, dgate_b), (dup_a, dup_b), (acc_a, acc_b)
    grads, sib = (grads_a, grads_b), (sib_a, sib_b)
    first, second, cross = (first_a, first_b), (second_a, second_b), (cross_a, cross_b)
    gd_out, gd_in = (gd_out_a, gd_out_b), (gd_in_a, gd_in_b)

    def columns(ref, s):
        return ref.at[:, pl.ds(*STAGES[s])]

    dp, owner = lax.axis_index("dp"), lax.axis_index("owner")
    y, zl, c = dp // 4, (dp // 2) % 2, dp % 2
    zc = dp % 4
    x, zh = owner // 4, owner % 4

    def dp_at(yy, z, cc):
        return (yy % 4) * 4 + z * 2 + cc

    peers = {
        "z": {"dp": dp_at(y, 1 - zl, c)},
        "up": {"dp": dp_at(y + 1, zl, c)},
        "down": {"dp": dp_at(y + 3, zl, c)},
        "sib": {"dp": dp_at(y, zl, 1 - c)},
        "x1": {"owner": ((x + 1) % 4) * 4 + zh},
        "x2": {"owner": ((x + 2) % 4) * 4 + zh},
        "x3": {"owner": ((x + 3) % 4) * 4 + zh},
        "zn": {"owner": x * 4 + (zh + 1) % 4},
        "zp": {"owner": x * 4 + (zh + 3) % 4},
        "z2": {"owner": x * 4 + (zh + 2) % 4},
    }
    turned = {"dp": y * 4 + zh, "owner": x * 4 + zc}
    moved = zh != zc

    load_tokens = pltpu.make_async_copy(tokens_hbm, tokens, tokens_sem)
    load_tokens.start()
    barrier = pltpu.get_barrier_semaphore()
    for target in peers.values():
        pl.semaphore_signal(barrier, inc=1, device_id=target, device_id_type=MESH)

    @pl.when(moved)
    def _():
        pl.semaphore_signal(barrier, inc=1, device_id=turned, device_id_type=MESH)

    down_t[...] = w_down[...].astype(F32).T.astype(BF)
    pl.semaphore_wait(barrier, len(peers) + moved.astype(jnp.int32))

    ids, sent = {}, []

    def index_of(name):
        return ids.setdefault(name, len(ids))

    def describe(name, src, dst, target):
        at = index_of(name)
        return pltpu.make_async_remote_copy(
            src_ref=src,
            dst_ref=dst,
            send_sem=send_sem.at[at],
            recv_sem=recv_sem.at[at],
            device_id=target,
            device_id_type=MESH,
        )

    def send(name, src, dst, peer):
        copy = describe(name, src, dst, peers[peer])
        copy.start()
        sent.append(copy)

    def arrived(name, dst):
        describe(name, dst, dst, peers["sib"]).wait_recv()

    def spread(w, tag, slot, peer, src=None):
        here = full[w[0]].at[w[1], slot]
        send(("w", w, tag), here if src is None else src, here, peer)

    def landed(w, tag, slot):
        arrived(("w", w, tag), full[w[0]].at[w[1], slot])

    mine = dp_at(y, zl, c)

    def spread0(w, own):
        for tag, peer in ((0, "up"), (1, "down"), (2, "z"), (3, "sib")):
            spread(w, tag, mine, peer, columns(own, w[0]))

    def spread1(w):
        slot = dp_at(y, 1 - zl, c)
        landed(w, 2, slot)
        for tag, peer in ((4, "up"), (5, "down"), (6, "sib")):
            spread(w, tag, slot, peer)

    def spread2(w):
        landed(w, 0, dp_at(y + 3, zl, c))
        landed(w, 4, dp_at(y + 3, 1 - zl, c))
        spread(w, 9, dp_at(y + 3, 0, c), "up")
        landed(w, 1, dp_at(y + 1, zl, c))
        landed(w, 5, dp_at(y + 1, 1 - zl, c))
        spread(w, 12, dp_at(y + 1, 1, c), "down")
        spread(w, 7, dp_at(y + 3, zl, c), "sib")
        spread(w, 8, dp_at(y + 3, 1 - zl, c), "sib")
        spread(w, 10, dp_at(y + 1, zl, c), "sib")
        spread(w, 11, dp_at(y + 1, 1 - zl, c), "sib")

    def spread3(w):
        landed(w, 9, dp_at(y + 2, 0, c))
        spread(w, 13, dp_at(y + 2, 0, c), "sib")
        landed(w, 12, dp_at(y + 2, 1, c))
        spread(w, 14, dp_at(y + 2, 1, c), "sib")

    def from_sibling(w, dy):
        o = 1 - c
        tags = {0: (3, 6), 3: (7, 8), 1: (10, 11), 2: (13, 14)}[dy]
        halves = (0, 1) if dy == 2 else (zl, 1 - zl)
        for tag, z in zip(tags, halves):
            landed(w, tag, dp_at(y + dy, z, o))

    def turn(name, src, dst):
        copy = describe(name, src, dst, turned)

        @pl.when(moved)
        def _():
            copy.start()

        return copy

    def turn_wait(copy, src, dst):
        @pl.when(moved)
        def _():
            copy.wait()

        @pl.when(jnp.logical_not(moved))
        def _():
            dst[...] = src[...]

    G1, U1, D1, G2, U2, D2 = [(stage, kind) for stage in (0, 1) for kind in (0, 1, DOWN)]
    spread0(G1, w_gate)
    turn_down = turn("turn_in", down_t, down_mine)
    for step in (1, 3, 2):
        send(("d", step), d_out, cot_all.at[x], "x%d" % step)
    cot_all[x] = d_out[...]
    for stage in (0, 1):
        full[stage][0, mine] = columns(w_gate, stage)[...]
        full[stage][1, mine] = columns(w_up, stage)[...]

    chosen = route[...]
    is_expert = lax.broadcasted_iota(jnp.int32, (8, ROWS), 0) == chosen
    upto = (
        lax.broadcasted_iota(jnp.int32, (ROWS, ROWS), 0)
        <= lax.broadcasted_iota(jnp.int32, (ROWS, ROWS), 1)
    )
    one, zero = jnp.float32(1.0), jnp.float32(0.0)
    counts = nn(jnp.where(is_expert, one, zero).astype(BF), jnp.where(upto, one, zero).astype(BF))
    place = jnp.where(is_expert, counts.astype(jnp.int32) - 1, -1)
    slot_ids = lax.broadcasted_iota(jnp.int32, (CAP, ROWS), 0)
    for e in range(4):
        chosen_slots = jnp.where(slot_ids == place[e : e + 1, :], one, zero).astype(BF)
        picks[e] = chosen_slots
        picks_t[e] = chosen_slots.T
    pick = picks.at[x]
    weight[...] = jnp.broadcast_to(
        jnp.sum(pick[...].astype(F32) * prob[...], axis=1, keepdims=True), (CAP, 128)
    )

    def token_slots(lo, hi):
        @pl.loop(lo, hi)
        def _(k):
            cols = pl.ds(pl.multiple_of(k * CH, CH), CH)
            value = nn(pick[...], tokens[:, cols]).astype(BF)
            slots[k] = value
            slots_t[k] = value.T

    def project(w, dy):
        out = (gate, up)[w[1]][w[0]]
        source = full[w[0]]
        base = 4 * ((y + dy) % 4)
        start = nn(slots[base], source[w[1], base])
        out[...] = start if dy == 0 else out[...] + start

        @pl.loop(1, 4)
        def _(j):
            out[...] += nn(slots[base + j], source[w[1], base + j])

    def project_all(w):
        for dy in (0, 3, 1, 2):
            from_sibling(w, dy)
            project(w, dy)

    half = CAP // 2
    nxt, prv, far = (zh + 1) % 4, (zh + 3) % 4, (zh + 2) % 4

    def hidden_term(s, p):
        total = acc[s]
        total[...] = nn(dexp[0], full[s][DOWN, p])

        @pl.loop(1, 4)
        def _(i):
            total[...] += nn(dexp[i], full[s][DOWN, 4 * i + p])

        dhid[s][p] = total[...].astype(BF)

    def hidden0(s):
        hidden_term(s, far)
        send(("h1n", s), dhid[s].at[far, pl.ds(0, half)], dh_first[s].at[0], "zn")
        send(("h1p", s), dhid[s].at[far, pl.ds(half, half)], dh_first[s].at[1], "zp")

    def hidden1(s):
        arrived(("h1n", s), dh_first[s].at[0])
        here = dhid[s].at[nxt, pl.ds(0, half)]
        add_rows(here, here, dh_first[s].at[0])
        send(("h2n", s), dhid[s].at[nxt], dh_second[s].at[0], "zn")
        arrived(("h1p", s), dh_first[s].at[1])
        here = dhid[s].at[prv, pl.ds(half, half)]
        add_rows(here, here, dh_first[s].at[1])
        send(("h2p", s), dhid[s].at[prv], dh_second[s].at[1], "zp")

    def activate(s):
        arrived(("h2n", s), dh_second[s].at[0])
        arrived(("h2p", s), dh_second[s].at[1])

        @pl.loop(0, CAP // 32)
        def _(step):
            at = pl.ds(pl.multiple_of(step * 32, 32), 32)
            g, u = gate[s][at, :], up[s][at, :]
            d = dhid[s][zh, at, :].astype(F32)
            d = d + dh_second[s][0, at, :].astype(F32) + dh_second[s][1, at, :].astype(F32)
            sig = jax.nn.sigmoid(g)
            active = g * sig
            hid[s][zh, at, :] = (active * u).astype(BF)
            dgate[s][at, :] = (d * u * sig * (1.0 + g * (1.0 - sig))).astype(BF)
            dup[s][at, :] = (d * active).astype(BF)

        send(("a1n", s), hid[s].at[zh], hid[s].at[zh], "zn")
        send(("a1p", s), hid[s].at[zh], hid[s].at[zh], "zp")

    def pass_hidden(s):
        arrived(("a1n", s), hid[s].at[prv])
        here = hid[s].at[prv, pl.ds(0, half)]
        send(("a2n", s), here, here, "zn")
        arrived(("a1p", s), hid[s].at[nxt])
        here = hid[s].at[nxt, pl.ds(half, half)]
        send(("a2p", s), here, here, "zp")

    def all_hidden(s):
        arrived(("a2n", s), hid[s].at[far, pl.ds(0, half)])
        arrived(("a2p", s), hid[s].at[far, pl.ds(half, half)])

    def input_term(d):
        @pl.loop(0, 4)
        def _(a):
            k = 4 * a + d
            total = nt(dgate_a[...], full_a[0, k]) + nt(dup_a[...], full_a[1, k])
            total = total + nt(dgate_b[...], full_b[0, k]) + nt(dup_b[...], full_b[1, k])
            part[d, a] = total.astype(BF)

    def input_send(tag, d):
        for step in (2, 1, 3):
            send(("g", tag, step), part.at[d, (x + step) % 4], g_in.at[d, x], "x%d" % step)
        g_in[d, x] = part[d, x]

    def back_to_rows(source, out):
        total = nn(picks_t[0], source[0])
        for e in range(1, 4):
            total = total + nn(picks_t[e], source[e])
        out[...] = total.astype(BF)

    def input_rows(tag, d):
        for step in (1, 3, 2):
            arrived(("g", tag, step), g_in.at[d, (x + 4 - step) % 4])
        back_to_rows(g_in.at[d], in_rows.at[d])

    def grad_term(w, core):
        s, kind = w

        @pl.loop(0, 8)
        def _(j):
            k = 2 * j + core
            if kind == DOWN:
                grads[s][kind, k] = nn(dexp_t[k // 4], hid[s][k % 4]).astype(BF)
            else:
                grads[s][kind, k] = nn(slots_t[k], (dgate, dup)[kind][s][...]).astype(BF)

    order = [(2, 0), (2, 1), (1, 0), (1, 1), (3, 0), (3, 1), (0, 0), (0, 1)]
    sides = ("up", "down")

    def grad_part(w, index, core):
        dy, z = order[index]
        return grads[w[0]].at[w[1], dp_at(y + dy, z, core)]

    def reduce0(w):
        grad_term(w, 1 - c)
        for index in range(8):
            here = sib[w[0]].at[w[1], index]
            send(("s", w, index), grad_part(w, index, 1 - c), here, "sib")

    def reduce1(w):
        grad_term(w, c)
        for index in (0, 1):
            here = sib[w[0]].at[w[1], index]
            arrived(("s", w, index), here)
            add_rows(here, here, grad_part(w, index, c))
            send(("t", w, index), here, first[w[0]].at[w[1], index], sides[index])

    def reduce2(w):
        for index in (2, 3, 4, 5):
            here = sib[w[0]].at[w[1], index]
            arrived(("s", w, index), here)
            side, z = (index - 2) // 2, index % 2
            if side == z:
                came = first[w[0]].at[w[1], side]
                arrived(("t", w, side), came)
                add_rows(here, here, grad_part(w, index, c), came)
            else:
                add_rows(here, here, grad_part(w, index, c))
            send(("t", w, index), here, second[w[0]].at[w[1], index - 2], sides[side])

    def reduce3(w):
        s, kind = w
        for index in (2, 3, 4, 5):
            arrived(("t", w, index), second[s].at[kind, index - 2])
        for index in (6, 7):
            arrived(("s", w, index), sib[s].at[kind, index])
        away = sib[s].at[kind, 7 - zl]
        add_rows(
            away,
            away,
            grads[s].at[kind, dp_at(y, 1 - zl, c)],
            second[s].at[kind, 1 - zl],
            second[s].at[kind, 3 - zl],
        )
        send(("c", w), away, cross[s].at[kind], "z")

    def reduce4(w):
        s, kind = w
        arrived(("c", w), cross[s].at[kind])
        add_rows(
            gd_out[s] if kind == DOWN else columns((grad_g, grad_u)[kind], s),
            sib[s].at[kind, 6 + zl],
            grads[s].at[kind, dp_at(y, zl, c)],
            second[s].at[kind, zl],
            second[s].at[kind, 2 + zl],
            cross[s].at[kind],
        )
        if kind == DOWN:
            return turn(("turn_out", s), gd_out[s], gd_in[s])

    def finish_down(s, copy):
        lo, width = STAGES[s]
        turn_wait(copy, gd_out[s], gd_in[s])
        grad_d[pl.ds(lo, width), :] = gd_in[s][...].astype(F32).T

    def layer_output():
        router[...] = jnp.zeros_like(router)

        @pl.loop(0, 4)
        def _(i):
            out = nt(hid_a[0], full_a[DOWN, 4 * i]) + nt(hid_b[0], full_b[DOWN, 4 * i])
            for p in range(1, 4):
                out = out + nt(hid_a[p], full_a[DOWN, 4 * i + p])
                out = out + nt(hid_b[p], full_b[DOWN, 4 * i + p])
            router[...] += jnp.broadcast_to(
                jnp.sum(cot[i].astype(F32) * out, axis=1, keepdims=True), (CAP, 128)
            )
            m_out[i] = (weight[:, 0:1] * out).astype(BF)

        for step in (1, 3, 2):
            send(("m", step), m_out.at[(x + step) % 4], m_in.at[x], "x%d" % step)
        r_z[zh] = jnp.broadcast_to(
            jnp.sum(pick[...].astype(F32) * router[:, 0:1], axis=0, keepdims=True), (8, ROWS)
        )
        for name in ("zn", "zp", "z2"):
            send(("r", name), r_z.at[zh], r_z.at[zh], name)
        m_in[x] = m_out[x]

    turn_wait(turn_down, down_t, down_mine)
    spread0(D1, down_mine)
    for stage in (0, 1):
        full[stage][DOWN, mine] = columns(down_mine, stage)[...]
    spread1(G1)
    spread0(U1, w_up)
    load_tokens.wait()
    token_slots(0, 8)
    spread1(D1)
    spread1(U1)
    token_slots(8, 16)
    spread2(D1)
    spread0(D2, down_mine)
    spread2(G1)
    for step in (1, 2, 3):
        arrived(("d", step), cot_all.at[(x + 4 - step) % 4])

    @pl.loop(0, 4)
    def _(i):
        value = nn(pick[...], cot_all[i])
        cot[i] = value.astype(BF)
        scaled = (weight[:, 0:1] * value).astype(BF)
        dexp[i] = scaled
        dexp_t[i] = scaled.T

    spread1(D2)
    spread0(G2, w_gate)
    spread3(D1)
    spread2(U1)
    for dy in range(4):
        from_sibling(D1, dy)
    hidden0(0)
    spread3(G1)
    hidden_term(0, nxt)
    hidden_term(0, prv)
    spread1(G2)
    spread0(U2, w_up)
    spread2(D2)
    spread3(U1)
    hidden1(0)
    project_all(G1)
    hidden_term(0, zh)
    spread1(U2)
    spread2(G2)
    project_all(U1)
    spread3(D2)
    for dy in range(4):
        from_sibling(D2, dy)
    hidden0(1)
    spread2(U2)
    hidden_term(1, nxt)
    hidden_term(1, prv)
    spread3(G2)
    activate(0)
    reduce0(G1)
    spread3(U2)
    reduce1(G1)
    hidden1(1)
    hidden_term(1, zh)
    project_all(G2)
    project_all(U2)
    activate(1)

    rh = ROWS // 2
    input_term(far)
    input_send(0, far)
    pass_hidden(0)
    reduce0(U1)
    input_term(nxt)
    input_send(1, nxt)
    reduce1(U1)
    reduce2(G1)
    pass_hidden(1)
    input_term(prv)
    input_send(2, prv)
    all_hidden(0)
    reduce0(D1)
    input_rows(0, far)
    send("g1n", in_rows.at[far, pl.ds(0, rh)], gz_a.at[0], "zn")
    send("g1p", in_rows.at[far, pl.ds(rh, rh)], gz_a.at[1], "zp")
    reduce1(D1)
    reduce2(U1)
    input_term(zh)
    input_send(3, zh)
    reduce0(G2)
    reduce1(G2)
    reduce0(U2)
    reduce1(U2)
    input_rows(1, nxt)
    arrived("g1n", gz_a.at[0])
    add_rows(in_rows.at[nxt, pl.ds(0, rh)], in_rows.at[nxt, pl.ds(0, rh)], gz_a.at[0])
    send("g2n", in_rows.at[nxt], gz_b.at[0], "zn")
    reduce3(G1)
    reduce2(D1)
    all_hidden(1)
    reduce0(D2)
    reduce1(D2)
    reduce2(G2)
    input_rows(2, prv)
    arrived("g1p", gz_a.at[1])
    add_rows(in_rows.at[prv, pl.ds(rh, rh)], in_rows.at[prv, pl.ds(rh, rh)], gz_a.at[1])
    send("g2p", in_rows.at[prv], gz_b.at[1], "zp")
    reduce3(U1)
    reduce2(U2)
    layer_output()
    reduce4(G1)
    reduce2(D2)
    reduce3(D1)
    reduce4(U1)
    for name, q in (("zn", prv), ("zp", nxt), ("z2", far)):
        arrived(("r", name), r_z.at[q])
    r_x[x] = r_z[0] + r_z[1] + r_z[2] + r_z[3]
    for step in (1, 3, 2):
        send(("q", step), r_x.at[x], r_x.at[x], "x%d" % step)
    reduce3(G2)
    turn_one = reduce4(D1)
    input_rows(3, zh)
    reduce3(U2)
    reduce4(G2)
    reduce3(D2)
    for step in (1, 2, 3):
        arrived(("m", step), m_in.at[(x + 4 - step) % 4])
    back_to_rows(m_in, mixed)
    reduce4(U2)
    turn_two = reduce4(D2)
    finish_down(0, turn_one)
    for step in (1, 2, 3):
        arrived(("q", step), r_x.at[(x + 4 - step) % 4])
    grad_gate[...] = (r_x[0] + r_x[1] + r_x[2] + r_x[3])[0:1, :]
    arrived("g2n", gz_b.at[0])
    arrived("g2p", gz_b.at[1])
    add_rows(grad_tokens, in_rows.at[zh], gz_b.at[0], gz_b.at[1])
    finish_down(1, turn_two)
    for copy in sent:
        copy.wait_send()


def hand_over(*refs):
    n = len(refs) // 3
    ins, outs, sems = refs[:n], refs[n : 2 * n], refs[3 * n]
    held = refs[2 * n : 3 * n]
    loads = [pltpu.make_async_copy(ins[i], held[i], sems.at[0, i]) for i in range(n)]
    stores = [pltpu.make_async_copy(held[i], outs[i], sems.at[1, i]) for i in range(n)]
    for load in loads:
        load.start()
    for load, store in zip(loads, stores):
        load.wait()
        store.start()
    for store in stores:
        store.wait()


def to_outputs(arrays):
    anywhere = pl.BlockSpec(memory_space=pl.ANY)
    return pl.pallas_call(
        hand_over,
        out_shape=tuple(jax.ShapeDtypeStruct(a.shape, a.dtype) for a in arrays),
        in_specs=[anywhere] * len(arrays),
        out_specs=(anywhere,) * len(arrays),
        scratch_shapes=[pltpu.VMEM(a.shape, a.dtype) for a in arrays]
        + [pltpu.SemaphoreType.DMA((2, len(arrays)))],
        compiler_params=pltpu.CompilerParams(vmem_limit_bytes=VMEM_LIMIT),
    )(*arrays)


def local(tokens, route, gate_prob, w_gate, w_up, w_down, d_out):
    vmem = pl.BlockSpec(memory_space=pltpu.VMEM)
    block = (CAP, CH)

    def staged(*shape, dtype=BF):
        return [pltpu.VMEM((*shape, width), dtype) for _, width in STAGES]

    results = pl.pallas_call(
        kernel,
        out_shape=(
            jax.ShapeDtypeStruct((ROWS, CH), BF),
            jax.ShapeDtypeStruct((ROWS, CH), BF),
            jax.ShapeDtypeStruct((1, ROWS), F32),
            jax.ShapeDtypeStruct((CH, PW), F32),
            jax.ShapeDtypeStruct((CH, PW), F32),
            jax.ShapeDtypeStruct((PW, CH), F32),
        ),
        in_specs=[pl.BlockSpec(memory_space=pl.ANY)] + [vmem] * 6,
        out_specs=(vmem,) * 6,
        scratch_shapes=[
            *staged(3, 16, CH),
            pltpu.VMEM((16, *block), BF),
            pltpu.VMEM((4, ROWS, CH), BF),
            pltpu.VMEM((4, *block), BF),
            pltpu.VMEM((4, *block), BF),
            *staged(4, CAP),
            *staged(2, CAP // 2),
            *staged(2, CAP),
            *staged(CAP, dtype=F32),
            *staged(CAP, dtype=F32),
            *staged(4, CAP),
            *staged(CAP),
            *staged(CAP),
            *staged(CAP, dtype=F32),
            pltpu.VMEM((4, 4, *block), BF),
            pltpu.VMEM((4, 4, *block), BF),
            pltpu.VMEM((4, ROWS, CH), BF),
            pltpu.VMEM((2, ROWS // 2, CH), BF),
            pltpu.VMEM((2, ROWS, CH), BF),
            pltpu.VMEM((4, *block), BF),
            pltpu.VMEM((4, *block), BF),
            *staged(3, 16, CH),
            *staged(3, 8, CH),
            *staged(3, 2, CH),
            *staged(3, 4, CH),
            *staged(3, CH),
            pltpu.VMEM((CH, PW), BF),
            pltpu.VMEM((CH, PW), BF),
            *staged(CH),
            *staged(CH),
            pltpu.VMEM((4, CAP, ROWS), BF),
            pltpu.VMEM((4, ROWS, CAP), BF),
            pltpu.VMEM((16, CH, CAP), BF),
            pltpu.VMEM((4, CH, CAP), BF),
            pltpu.VMEM((CAP, 128), F32),
            pltpu.VMEM((CAP, 128), F32),
            pltpu.VMEM((4, 8, ROWS), F32),
            pltpu.VMEM((4, 8, ROWS), F32),
            pltpu.VMEM((ROWS, 16 * CH), BF),
            pltpu.SemaphoreType.DMA,
            pltpu.SemaphoreType.DMA((COPIES,)),
            pltpu.SemaphoreType.DMA((COPIES,)),
        ],
        compiler_params=pltpu.CompilerParams(
            collective_id=0, has_side_effects=True, vmem_limit_bytes=VMEM_LIMIT
        ),
    )(tokens, route.reshape(1, ROWS), gate_prob.reshape(1, ROWS), w_gate, w_up, w_down, d_out)
    mixed, grad_tokens, grad_gate, grad_g, grad_u, grad_d = to_outputs(results)
    return (mixed, grad_tokens, grad_gate.reshape(ROWS), grad_g, grad_u, grad_d)


def solution(mesh):
    in_specs = (
        P("dp", None),
        P("dp", None),
        P("dp"),
        P("dp", "owner"),
        P("dp", "owner"),
        P("owner", "dp"),
        P("dp", "owner"),
    )
    out_specs = (
        P("dp", "owner"),
        P("dp", "owner"),
        P("dp"),
        P("dp", "owner"),
        P("dp", "owner"),
        P("owner", "dp"),
    )
    return jax.shard_map(local, mesh=mesh, in_specs=in_specs, out_specs=out_specs, check_vma=False)
```
